32 devices in a mesh: dp: 16 (over z, y, x), tensor: 2 (over core).
Axes of the slice: x: 2, y: 2, z: 4, core: 2. Of those that a mesh axis runs over, the one named last changes fastest.
Arguments:
- hidden: bfloat16 [128, 4096], P('dp'), may hold values from -20 to 20
- gain: bfloat16 [4096], replicated, may hold values from 0.5 to 1.5
- head: bfloat16 [4096, 4096], P(('dp', 'tensor')), may hold values from -32 to 32
- moment: bfloat16 [4096, 4096], P(('dp', 'tensor')), may hold values from -6 to 6
- second: float32 [4096], P(('dp', 'tensor')), may hold values from 0.5 to 50
- labels: int32 [128], P('dp'), may hold values from 0 to 4095
Outputs:
- grad_hidden: bfloat16 [128, 4096], P('dp')
- grad_gain: float32 [4096], replicated
- head_new: bfloat16 [4096, 4096], P(('dp', 'tensor'))
- moment_new: bfloat16 [4096, 4096], P(('dp', 'tensor'))
- second_new: float32 [4096], P(('dp', 'tensor'))
The draws below stay inside these ranges and needn't reach their ends.
All inputs are finite; a program needn't handle non-finite values.
Results may differ from the reference program's by a relative error of at most 0.01.
Values may be sent and summed in bfloat16 or wider, within the bound.
A program may use at most 64 MiB of HBM per device.

```python
import math
import jax
import jax.numpy as jnp
from jax import lax

D = 4096
ROWS_OWN = 128
VOCAB = 4096
TOKENS = 128
N_DP = 16
N_TENSOR = 2


def pair_vectors(key):
    return jax.random.normal(jax.random.fold_in(key, 7), (4, D), jnp.float32)


def draw_hidden(key, part):
    own_key = jax.random.fold_in(key, 11)
    values = jnp.clip(jax.random.normal(own_key, (TOKENS, D), jnp.float32), -6.0, 6.0)
    aligned = jnp.clip(pair_vectors(key), -5.0, 5.0)
    values = jnp.concatenate([aligned, values[4:]], 0)
    return values.astype(jnp.bfloat16)


def draw_head(key, part):
    own_key = jax.random.fold_in(key, 13)
    sigma = 3.0 / math.sqrt(D)
    values = jnp.clip(sigma * jax.random.normal(own_key, (VOCAB, D), jnp.float32), -6.0 * sigma, 6.0 * sigma)
    aligned = jnp.clip(pair_vectors(key), -5.0, 5.0)
    strength = jnp.array([2.0, 3.0, 4.0, 5.0], jnp.float32)
    upper = aligned * (64.0 * strength[:, None]) / D + 0.3 * sigma * jax.random.normal(jax.random.fold_in(own_key, 3), (4, D), jnp.float32)
    lower = aligned * (64.0 * strength[:, None] - 2.0) / D + 0.3 * sigma * jax.random.normal(jax.random.fold_in(own_key, 4), (4, D), jnp.float32)
    paired = jnp.stack([upper, lower], 1).reshape(8, D)
    values = jnp.concatenate([paired, values[8:]], 0)
    return jnp.clip(values, -32.0, 32.0).astype(jnp.bfloat16)


def with_ends(entries, stream_key, least, largest):
    extent = entries.shape
    place = [jax.random.randint(jax.random.fold_in(stream_key, axis), (), 0, extent[axis]) for axis in range(len(extent))]
    entries = entries.at[tuple(place)].set(least)
    longest = extent.index(max(extent))
    place[longest] = (place[longest] + 1) % extent[longest]
    return entries.at[tuple(place)].set(largest)


def block_scale(key, dims, split, least, high):
    def one(axis_at, shards_of):
        steps = jax.random.uniform(jax.random.fold_in(jax.random.fold_in(key, 6), axis_at), (shards_of,), jnp.float32, least / len(split), high / len(split))
        return jnp.repeat(jnp.exp(steps), dims[axis_at] // shards_of).reshape((-1,) + (1,) * (len(dims) - axis_at - 1))

    level = one(*split[0])
    for cut in split[1:]:
        level = level * one(*cut)
    return level


def bell_draw(key, dims, scale, limit, shards=(), held_as=jnp.bfloat16):
    entries = jax.random.normal(key, dims, jnp.float32) * scale
    if len(shards) > 0:
        entries = block_scale(key, dims, shards, -0.22, 0.18) * entries
    return jnp.clip(entries, min=-limit, max=limit).astype(held_as)


def setup_inputs(seed: int = 0) -> dict:
    key_list = jax.random.split(jax.random.key(seed), 7)
    hidden = draw_hidden(jax.random.fold_in(key_list[6], 71), 0)
    gain = jnp.clip(1.0 + 0.1 * jax.random.normal(key_list[1], (D,), jnp.float32), 0.5, 1.5).astype(jnp.bfloat16)
    head = draw_head(jax.random.fold_in(key_list[6], 71), 0)
    moment = bell_draw(key_list[3], (VOCAB, D), 1.0, 6.0, ((0, 32),))
    second = jnp.clip(jnp.exp(math.log(50.0) - 4.6051702 * jax.random.uniform(key_list[4], (VOCAB,), jnp.float32) ** block_scale(key_list[4], (VOCAB,), ((0, 32),), -0.2, 0.2)), 0.5, 50.0)
    labels = with_ends(jax.random.randint(key_list[5], (TOKENS,), 0, VOCAB), jax.random.fold_in(key_list[5], 1), 0, VOCAB - 1).astype(jnp.int32)
    return {"hidden": hidden, "gain": gain, "head": head, "moment": moment, "second": second, "labels": labels}


loss_scale = 16.0
beta_one = 0.9
beta_two = 0.999
adam_eps = 1e-08
step_size = 0.02
norm_eps = 1e-05
bias_one = 1.0 - 0.9 ** 10
bias_two = 1.0 - 0.999 ** 10

def reference(hidden, gain, head, moment, second, labels):
    hidden_f = hidden.astype(jnp.float32)
    gain_f = gain.astype(jnp.float32)
    squares = lax.optimization_barrier(jnp.sum(hidden_f * hidden_f, axis=1))
    rstd = lax.rsqrt(squares / D + norm_eps)
    normed = (hidden_f * rstd[:, None] * gain_f).astype(jnp.bfloat16)
    block_rows = ROWS_OWN * N_TENSOR
    blocks = head.reshape(N_DP, block_rows, D)
    block_ids = jnp.arange(VOCAB, dtype=jnp.int32).reshape(N_DP, block_rows)

    def stats_step(running, window):
        run_max, run_sum = running
        logits = jnp.dot(normed, window.T, preferred_element_type=jnp.float32)
        new_max = jnp.maximum(run_max, lax.optimization_barrier(jnp.max(logits, axis=1)))
        new_sum = run_sum * jnp.exp(run_max - new_max) + lax.optimization_barrier(jnp.sum(jnp.exp(logits - new_max[:, None]), axis=1))
        return ((new_max, new_sum), None)
    start_max = jnp.full((TOKENS,), -1e+30, jnp.float32)
    start_sum = jnp.zeros((TOKENS,), jnp.float32)
    (row_max, row_sum), _ = lax.scan(stats_step, (start_max, start_sum), blocks)

    def grad_step(grad_acc, inputs):
        window, vocab_ids = inputs
        logits = jnp.dot(normed, window.T, preferred_element_type=jnp.float32)
        onehot = (labels[:, None] == vocab_ids[None, :]).astype(jnp.float32)
        probability = jnp.exp(logits - row_max[:, None]) / row_sum[:, None]
        dlogits = (loss_scale * (probability - onehot)).astype(jnp.bfloat16)
        grad_window = jnp.dot(dlogits.T, normed, preferred_element_type=jnp.float32)
        split_logits = dlogits.reshape(TOKENS, N_TENSOR, ROWS_OWN).astype(jnp.float32)
        split_rows = window.reshape(N_TENSOR, ROWS_OWN, D).astype(jnp.float32)
        partials = jnp.einsum('tkr,krd->ktd', split_logits, split_rows).astype(jnp.bfloat16)
        grad_acc = grad_acc + lax.optimization_barrier(jnp.sum(partials.astype(jnp.float32), axis=0))
        return (grad_acc, grad_window)
    grad_start = jnp.zeros((TOKENS, D), jnp.float32)
    grad_normed, grad_windows = lax.scan(grad_step, grad_start, (blocks, block_ids))
    grad_head = grad_windows.reshape(VOCAB, D)
    grad_gain = lax.optimization_barrier(jnp.sum(grad_normed * hidden_f * rstd[:, None], axis=0))
    inner_sums = lax.optimization_barrier(jnp.sum(grad_normed * gain_f * hidden_f, axis=1))
    grad_hidden = (rstd[:, None] * gain_f * grad_normed - hidden_f * (rstd ** 3)[:, None] * inner_sums[:, None] / D).astype(jnp.bfloat16)
    second_new = beta_two * second + (1.0 - beta_two) * lax.optimization_barrier(jnp.sum(grad_head * grad_head, axis=1)) / D
    first = beta_one * moment.astype(jnp.float32) + (1.0 - beta_one) * grad_head
    adam_step = first / bias_one / (jnp.sqrt(second_new / bias_two)[:, None] + adam_eps)
    head_new = (head.astype(jnp.float32) - step_size * adam_step).astype(jnp.bfloat16)
    return (grad_hidden, grad_gain, head_new, first.astype(jnp.bfloat16), second_new)
```

```python
import functools

import jax
import jax.numpy as jnp
from jax import lax
from jax.experimental import pallas as pl
from jax.experimental.pallas import tpu as pltpu
from jax.sharding import PartitionSpec as P

MESH = pl.DeviceIdType.MESH
LANES = 128
PLANE = 4
CHUNK = 512
PIECES = 4
STEPS = (3, 1, 2)
CHUNKS = ((0,), (1, 2, 3))
FAR_FIRST = tuple(sorted(range(1, 16), key=lambda step: -min(step, 16 - step)))
VMEM_BYTES = 40 * 1024 * 1024

D = 4096


loss_scale = 16.0
beta_one = 0.9
beta_two = 0.999
adam_eps = 1e-08
step_size = 0.02
norm_eps = 1e-05
bias_one = 1.0 - 0.9**10
bias_two = 1.0 - 0.999**10


def inverse_norm(values_f):
    squares = jnp.sum(values_f * values_f, axis=1)
    return lax.rsqrt(squares / D + norm_eps)


def softmax_grad(logits, targets, vocab_ids):
    local_max = jnp.max(logits, axis=1)
    local_sum = jnp.sum(jnp.exp(logits - local_max[:, None]), axis=1)
    global_max = lax.pmax(local_max, ("dp", "tensor"))
    global_sum = lax.psum(local_sum * jnp.exp(local_max - global_max), ("dp", "tensor"))
    onehot = (targets[:, None] == vocab_ids[None, :]).astype(jnp.float32)
    probability = jnp.exp(logits - global_max[:, None]) / global_sum[:, None]
    return (loss_scale * (probability - onehot)).astype(jnp.bfloat16)


def norm_backward(grad_normed, hidden_part, rstd_part, gain_f):
    inner_sums = jnp.sum(grad_normed * gain_f * hidden_part, axis=1)
    return (
        rstd_part[:, None] * gain_f * grad_normed
        - hidden_part * (rstd_part**3)[:, None] * inner_sums[:, None] / D
    ).astype(jnp.bfloat16)


def local(hidden, gain, head, moment, second, labels):
    hidden_f = hidden.astype(jnp.float32)
    gain_f = gain.astype(jnp.float32)
    rstd = inverse_norm(hidden_f)
    normed = (hidden_f * rstd[:, None] * gain_f).astype(jnp.bfloat16)
    normed_all = lax.all_gather(normed, "dp", axis=0, tiled=True)
    all_labels = lax.all_gather(labels, "dp", axis=0, tiled=True)
    own_rows = head.shape[0]
    tensor_count = lax.axis_size("tensor")
    dp_count = lax.axis_size("dp")
    owner = lax.axis_index("dp") * tensor_count + lax.axis_index("tensor")
    vocab_ids = owner * own_rows + jnp.arange(own_rows, dtype=jnp.int32)
    logits = lax.dot_general(
        normed_all, head, (((1,), (1,)), ((), ())), preferred_element_type=jnp.float32
    )
    dlogits = softmax_grad(logits, all_labels, vocab_ids)
    grad_head = lax.dot_general(
        dlogits, normed_all, (((0,), (0,)), ((), ())), preferred_element_type=jnp.float32
    )
    share_rows = hidden.shape[0] // tensor_count
    ordered = dlogits.reshape(dp_count, tensor_count, share_rows, own_rows).transpose(1, 0, 2, 3)
    ordered = ordered.reshape(tensor_count * dp_count * share_rows, own_rows)
    tensor_sum = lax.psum_scatter(
        jnp.dot(ordered, head, preferred_element_type=jnp.float32).astype(jnp.bfloat16),
        "tensor",
        scatter_dimension=0,
        tiled=True,
    ).astype(jnp.float32)
    full_sum = lax.psum(tensor_sum, "dp")
    grad_normed = lax.dynamic_slice_in_dim(
        full_sum, lax.axis_index("dp") * share_rows, share_rows, 0
    )
    offset = lax.axis_index("tensor") * share_rows
    hidden_part = lax.dynamic_slice_in_dim(hidden_f, offset, share_rows, 0)
    rstd_part = lax.dynamic_slice_in_dim(rstd, offset, share_rows, 0)
    grad_gain = lax.psum(
        jnp.sum(grad_normed * hidden_part * rstd_part[:, None], axis=0), ("dp", "tensor")
    )
    part_grad = norm_backward(grad_normed, hidden_part, rstd_part, gain_f)
    grad_hidden = lax.all_gather(part_grad, "tensor", axis=0, tiled=True)
    row_sums = jnp.sum(grad_head * grad_head, axis=1)
    second_new = beta_two * second + (1.0 - beta_two) * row_sums / D
    first = beta_one * moment.astype(jnp.float32) + (1.0 - beta_one) * grad_head
    adam_step = first / bias_one / (jnp.sqrt(second_new / bias_two)[:, None] + adam_eps)
    head_new = (head.astype(jnp.float32) - step_size * adam_step).astype(jnp.bfloat16)
    return (grad_hidden, grad_gain, head_new, first.astype(jnp.bfloat16), second_new)


def wide(values):
    return values.astype(jnp.float32)


def narrow(values):
    return values.astype(jnp.bfloat16)


def fused_kernel(
    layers,
    hidden_hbm,
    gain_hbm,
    head_hbm,
    moment_hbm,
    second_hbm,
    labels_hbm,
    grad_hidden_ref,
    grad_gain_ref,
    head_new,
    moment_new,
    second_out,
    gathered,
    hidden,
    gain,
    heads,
    moment,
    second,
    labels,
    gain_wide,
    rates,
    logits_acc,
    grad_head,
    stat_out,
    stat_in,
    token_rows,
    by_token,
    plane_out,
    plane_in,
    plane_sum,
    line_out,
    line_in,
    final,
    gain_out,
    gain_in,
    gain_all,
    local_sems,
    head_sems,
    gather_recv,
    gather_line,
    gather_plane,
    gather_pair,
    stat_send,
    stat_recv,
    plane_sems,
    line_send,
    line_recv,
    final_send,
    final_recv,
    gain_send,
    gain_recv,
    share_send,
    share_recv,
):
    groups = layers * PLANE
    own_tokens, width = hidden.shape
    own_rows = moment.shape[0]
    virtual = groups * 2 * own_tokens
    piece = width // PIECES
    half = piece // 2
    dp = lax.axis_index("dp")
    core = lax.axis_index("tensor")
    layer = lax.div(dp, PLANE)
    spot = lax.rem(dp, PLANE)
    flip = lax.div(layer, 2)
    inward = layer + flip * (3 - 2 * layer)
    pieces = range(PIECES)

    def hop(item):
        if item == layers - 1:
            return layer
        place = 1 - inward if item == 0 else item + 1
        return place + flip * (3 - 2 * place)

    def beside(step):
        down = lax.rem(lax.div(spot, 2) + step // 2, 2)
        return down * 2 + lax.rem(lax.rem(spot, 2) + step % 2, 2)

    def remote(source, target, send_sem, recv_sem, device):
        return pltpu.make_async_remote_copy(
            src_ref=source,
            dst_ref=target,
            send_sem=send_sem,
            recv_sem=recv_sem,
            device_id=device,
            device_id_type=MESH,
        )

    barrier = pltpu.get_barrier_semaphore()
    for item in (2, 1, 0):
        pl.semaphore_signal(
            barrier, inc=1, device_id=(hop(item) * PLANE + spot, core), device_id_type=MESH
        )
    for step in STEPS:
        pl.semaphore_signal(
            barrier, inc=1, device_id=(layer * PLANE + beside(step), core), device_id_type=MESH
        )
    pl.semaphore_signal(barrier, inc=1, device_id=(dp, 1 - core), device_id_type=MESH)

    loads = [
        pltpu.make_async_copy(source, target, local_sems.at[index])
        for index, (source, target) in enumerate(
            [
                (hidden_hbm, hidden),
                (gain_hbm, gain),
                (head_hbm, heads.at[core]),
                (labels_hbm, labels),
                (moment_hbm, moment),
                (second_hbm, second),
            ]
        )
    ]
    for load in loads:
        load.start()

    def run(me):
        you = 1 - me
        chunks = CHUNKS[me]
        sends = []

        def send(*parts):
            copy = remote(*parts)
            copy.start()
            sends.append(copy)

        loads[0].wait()
        loads[1].wait()
        gain_rows = wide(gain[...])
        for row in range(width // LANES):
            gain_wide[:, row * LANES : (row + 1) * LANES] = gain_rows[row : row + 1]
        hidden_f = wide(hidden[...])
        rstd = lax.rsqrt(jnp.sum(hidden_f * hidden_f, axis=1, keepdims=True) / width + norm_eps)
        own = hidden_f * rstd * gain_wide[...]
        rates[...] = jnp.broadcast_to(rstd, rates.shape)
        for part in pieces:
            at = part * piece
            gathered[part, dp] = narrow(
                jnp.concatenate([own[:, at : at + half], own[:, at + half : at + piece]], axis=0)
            )
        pl.semaphore_wait(barrier, layers - 1 + len(STEPS) + 1)

        def group_of(item, step=0):
            return hop(item) * PLANE + (beside(step) if step else spot)

        def shard(part, group, send_sem, device):
            block = gathered.at[part, group]
            return block, block, send_sem, gather_recv.at[part, group], device

        def arrived(part, group):
            block = gathered.at[part, group]
            remote(
                block, block, gather_pair.at[part, group], gather_recv.at[part, group], (dp, you)
            ).wait_recv()

        def plane_shards(part, item):
            for step in STEPS:
                send(
                    *shard(
                        part,
                        group_of(item),
                        gather_plane.at[part, item, step],
                        (layer * PLANE + beside(step), me),
                    )
                )

        def pair_shard(part, group):
            send(*shard(part, group, gather_pair.at[part, group], (dp, you)))

        def add_logits(part):
            block = gathered[part].reshape(virtual, half)
            for side in range(2):
                at = part * piece + side * half
                product = lax.dot_general(
                    heads[:, :, at : at + half].reshape(2 * own_rows, half),
                    block,
                    (((1,), (1,)), ((), ())),
                    preferred_element_type=jnp.float32,
                )
                if part == 0:
                    logits_acc[side] = product
                else:
                    logits_acc[side] = logits_acc[side] + product

        head_copy = (
            heads.at[me],
            heads.at[me],
            head_sems.at[0],
            head_sems.at[1],
            (dp, you),
        )
        head_in = remote(
            heads.at[you], heads.at[you], head_sems.at[0], head_sems.at[1], (dp, you)
        )
        if me == 1:
            for part in pieces:
                for item in (2, 1, 0):
                    send(
                        *shard(
                            part, dp, gather_line.at[part, item], (hop(item) * PLANE + spot, me)
                        )
                    )
            for part in pieces:
                plane_shards(part, 3)
            loads[2].wait()
            send(*head_copy)
            for part in pieces:
                for item in range(layers - 1):
                    arrived(part, group_of(item))
                    plane_shards(part, item)
                    pair_shard(part, group_of(item))
            for part in pieces:
                for item in (3, 0, 1, 2):
                    for step in STEPS:
                        arrived(part, group_of(item, step))
                        pair_shard(part, group_of(item, step))
                if part == 0:
                    head_in.wait_recv()
                add_logits(part)
        else:
            loads[2].wait()
            send(*head_copy)
            for part in pieces:
                for item in (3, 0, 1, 2):
                    for step in (0,) + STEPS:
                        if item < 3 or step:
                            arrived(part, group_of(item, step))
                if part == 0:
                    head_in.wait_recv()
                add_logits(part)

        logits = logits_acc[0] + pltpu.roll(logits_acc[1], virtual - own_tokens, 1)
        lane = lax.broadcasted_iota(jnp.int32, (1, virtual), 1)
        valid = lax.rem(lane, 2 * own_tokens) < own_tokens

        def stat_move(group, to_core, slot):
            return (
                stat_out.at[pl.ds(0, 4)],
                stat_in.at[dp, pl.ds(0, 4)],
                stat_send.at[slot],
                stat_recv.at[dp],
                (group, to_core),
            )

        if me == 1:
            loads[3].wait()
            local_max = jnp.max(logits, axis=0, keepdims=True)
            local_sum = jnp.sum(jnp.exp(logits - local_max), axis=0, keepdims=True)
            targets = jnp.zeros((1, virtual), jnp.int32)
            for item in range(own_tokens):
                targets = jnp.where(
                    lane == dp * 2 * own_tokens + item, labels[item], targets
                )
            packed = jnp.where(valid, local_max, pltpu.roll(local_sum, own_tokens, 1))
            targets = wide(targets)
            for row in range(2):
                span = slice(row * LANES, (row + 1) * LANES)
                stat_out[row : row + 1] = packed[:, span]
                stat_out[row + 2 : row + 3] = targets[:, span]
            for step in FAR_FIRST:
                group = lax.rem(dp + step, groups)
                send(*stat_move(group, 1, 2 * step + 1))
            for step in FAR_FIRST:
                group = lax.rem(dp + step, groups)
                send(*stat_move(group, 0, 2 * step))
            send(*stat_move(dp, 0, 0))
            stat_in[dp, 0:4] = stat_out[0:4]
        for step in range(groups):
            if me == 0 or step:
                group = lax.rem(dp + step, groups)
                slot = stat_in.at[group, pl.ds(0, 4)]
                remote(
                    slot, slot, stat_send.at[0], stat_recv.at[group], (dp, you)
                ).wait_recv()
        packets = [stat_in[group, 0:4] for group in range(groups)]
        peak = packets[0]
        for item in packets[1:]:
            peak = jnp.maximum(peak, item)
        total = jnp.zeros_like(peak)
        ids = jnp.zeros_like(peak)
        for item in packets:
            total = total + pltpu.roll(item, LANES - own_tokens, 1) * jnp.exp(item - peak)
            ids = ids + item

        def spread(values, row):
            return jnp.concatenate([values[row : row + 1], values[row + 1 : row + 2]], axis=1)

        global_max = spread(peak, 0)
        global_sum = jnp.where(valid, spread(total, 0), 1.0)
        all_targets = spread(ids, 2).astype(jnp.int32)
        vocab = dp * 2 * own_rows + lax.broadcasted_iota(jnp.int32, logits.shape, 0)
        onehot = wide(vocab == all_targets)
        probability = jnp.exp(logits - global_max) / global_sum
        scaled = jnp.where(valid, loss_scale * (probability - onehot), 0.0)
        turned = scaled.T.reshape(groups, 2, own_tokens, 2 * own_rows)
        for group in range(groups):
            token_rows[group] = turned[group, 0]
        for index, step in enumerate(STEPS + (0,)):
            blocks = [
                token_rows[hop(item) * PLANE + beside(step)] for item in range(layers)
            ]
            rows = layers * own_tokens
            by_token[index * rows : (index + 1) * rows] = narrow(jnp.concatenate(blocks, axis=0))

        def plane_parts(chunk, index):
            return (
                plane_out.at[chunk, index],
                plane_in.at[chunk, index],
                plane_sems.at[0, chunk, index],
                plane_sems.at[1, chunk, index],
                (layer * PLANE + beside(STEPS[index]), me),
            )

        rows = layers * own_tokens
        for chunk in chunks:
            for side in range(2):
                at = chunk * piece + side * half
                span = slice(side * half, (side + 1) * half)
                partial = jnp.dot(
                    by_token[...],
                    heads[:, :, at : at + half].reshape(2 * own_rows, half),
                    preferred_element_type=jnp.float32,
                )
                for index in range(len(STEPS)):
                    plane_out[chunk, index, :, span] = narrow(
                        partial[index * rows : (index + 1) * rows]
                    )
                plane_sum[chunk, :, span] = partial[len(STEPS) * rows :]
            for index in range(len(STEPS)):
                send(*plane_parts(chunk, index))

        mine = scaled[me * own_rows : (me + 1) * own_rows]
        by_row = (narrow(mine), narrow(pltpu.roll(mine, own_tokens, 1)))
        squares = jnp.zeros((own_rows, 1), jnp.float32)
        for part in pieces:
            block = gathered[part].reshape(virtual, half)
            for side in range(2):
                at = part * piece + side * half
                product = jnp.dot(by_row[side], block, preferred_element_type=jnp.float32)
                grad_head[:, at : at + half] = product
                squares = squares + jnp.sum(product * product, axis=1, keepdims=True)
                shares = jnp.sum(product * wide(heads[me, :, at : at + half]), axis=0, keepdims=True)
                shares = shares / gain_wide[:, at : at + half]
                for line in range(half // LANES):
                    place = at // LANES + line
                    gain_out[place // 2, place % 2 : place % 2 + 1] = shares[
                        :, line * LANES : (line + 1) * LANES
                    ]

        def gain_parts(group):
            return (
                gain_out.at[group],
                gain_in.at[me, dp],
                gain_send.at[group],
                gain_recv.at[me, dp],
                (group, 1),
            )

        for step in FAR_FIRST:
            send(*gain_parts(lax.rem(dp + step, groups)))
        if me == 0:
            send(*gain_parts(dp))
        else:
            gain_in[me, dp] = gain_out[dp]

        loads[4].wait()
        loads[5].wait()
        second_wide = jnp.broadcast_to(second[...], (LANES, own_rows)).T
        second_new = beta_two * second_wide + (1.0 - beta_two) * squares / width
        second_out[...] = second_new.T[0:1, :]
        scale = (step_size / bias_one) / (jnp.sqrt(second_new / bias_two) + adam_eps)
        scale = scale[:, 0:1]

        def adam(index, carry):
            span = pl.ds(pl.multiple_of(index * CHUNK, CHUNK), CHUNK)
            first = beta_one * wide(moment[:, span]) + (1.0 - beta_one) * grad_head[:, span]
            moment_new[:, span] = narrow(first)
            head_new[:, span] = narrow(wide(heads[me, :, span]) - first * scale)
            return carry

        lax.fori_loop(0, width // CHUNK, adam, 0)

        def line_parts(chunk, item):
            return (
                line_out.at[chunk, item],
                line_in.at[chunk, layer],
                line_send.at[chunk, item],
                line_recv.at[chunk, layer],
                (hop(item) * PLANE + spot, me),
            )

        for chunk in chunks:
            total = plane_sum[chunk]
            for index in range(len(STEPS)):
                remote(*plane_parts(chunk, index)).wait_recv()
                total = total + wide(plane_in[chunk, index])
            for item in (2, 1, 0):
                part = total[item * own_tokens : (item + 1) * own_tokens]
                line_out[chunk, item] = narrow(
                    jnp.concatenate([part[:, :half], part[:, half:]], axis=0)
                )
                send(*line_parts(chunk, item))
            final[chunk] = total[(layers - 1) * own_tokens :]

        def share_parts(group, to_core, slot):
            return (
                gain_all.at[dp],
                gain_all.at[dp],
                share_send.at[slot],
                share_recv.at[dp],
                (group, to_core),
            )

        if me == 1:
            for source in range(2):
                for step in range(groups):
                    if step or source == 0:
                        group = lax.rem(dp + step, groups)
                        slot = gain_in.at[source, group]
                        remote(
                            slot, slot, gain_send.at[0], gain_recv.at[source, group], (dp, you)
                        ).wait_recv()
            gain_all[dp] = jnp.sum(
                gain_in[...].reshape(2 * groups, 2, LANES), axis=0
            )
            for step in FAR_FIRST:
                group = lax.rem(dp + step, groups)
                send(*share_parts(group, 1, 2 * step + 1))
                send(*share_parts(group, 0, 2 * step))
            send(*share_parts(dp, 0, 0))

        def final_parts(chunk):
            return (
                final.at[chunk],
                final.at[chunk],
                final_send.at[chunk],
                final_recv.at[chunk],
                (dp, you),
            )

        for chunk in chunks:
            total = final[chunk]
            for item in range(layers - 1):
                source = hop(item)
                slot = line_in.at[chunk, source]
                remote(
                    slot, slot, line_send.at[chunk, item], line_recv.at[chunk, source], (dp, you)
                ).wait_recv()
                part = wide(line_in[chunk, source])
                total = total + jnp.concatenate(
                    [part[:own_tokens], part[own_tokens:]], axis=1
                )
            final[chunk] = total
            send(*final_parts(chunk))
        for step in range(groups):
            if me == 0 or step:
                group = lax.rem(dp + step, groups)
                slot = gain_all.at[group]
                remote(
                    slot, slot, share_send.at[0], share_recv.at[group], (dp, you)
                ).wait_recv()
        grad_gain_ref[...] = gain_all[...].reshape(width // LANES, LANES)
        for chunk in CHUNKS[you]:
            remote(*final_parts(chunk)).wait_recv()
        summed = jnp.concatenate([final[chunk] for chunk in pieces], axis=1) * gain_wide[...]
        hidden_f = wide(hidden[...])
        rstd = rates[:, 0:1]
        inner = jnp.sum(summed * hidden_f, axis=1, keepdims=True)
        grad_hidden_ref[...] = narrow(
            rstd * summed - hidden_f * (rstd * rstd * rstd * inner / width)
        )
        if me == 0:
            loads[3].wait()
        for copy in sends:
            copy.wait_send()

    for index in range(2):
        pl.when(core == index)(functools.partial(run, index))


def fused(groups, hidden, gain, head, moment, second, labels):
    own_tokens, width = hidden.shape
    own_rows = head.shape[0]
    layers = groups // PLANE
    tokens = groups * own_tokens
    virtual = 2 * tokens
    piece = width // PIECES
    half = piece // 2
    lines = width // LANES
    bf16, f32 = jnp.bfloat16, jnp.float32
    vmem = pl.BlockSpec(memory_space=pltpu.VMEM)
    hbm = pl.BlockSpec(memory_space=pltpu.HBM)
    dma = pltpu.SemaphoreType.DMA
    operands = (
        hidden,
        gain.reshape(lines, LANES),
        head,
        moment,
        second.reshape(1, own_rows),
        labels,
    )
    steps = len(STEPS)
    results = pl.pallas_call(
        functools.partial(fused_kernel, layers),
        out_shape=(
            pltpu.VMEM(hidden.shape, bf16),
            pltpu.VMEM((lines, LANES), f32),
            pltpu.VMEM(head.shape, bf16),
            pltpu.VMEM(head.shape, bf16),
            pltpu.VMEM((1, own_rows), f32),
        ),
        in_specs=[hbm] * len(operands),
        out_specs=(vmem,) * 5,
        scratch_shapes=[
            pltpu.VMEM((PIECES, groups, 2 * own_tokens, half), bf16),
            pltpu.VMEM(hidden.shape, bf16),
            pltpu.VMEM((lines, LANES), bf16),
            pltpu.VMEM((2, own_rows, width), bf16),
            pltpu.VMEM((own_rows, width), bf16),
            pltpu.VMEM((1, own_rows), f32),
            pltpu.SMEM((own_tokens,), jnp.int32),
            pltpu.VMEM((1, width), f32),
            pltpu.VMEM((own_tokens, LANES), f32),
            pltpu.VMEM((2, 2 * own_rows, virtual), f32),
            pltpu.VMEM((own_rows, width), f32),
            pltpu.VMEM((8, LANES), f32),
            pltpu.VMEM((groups, 8, LANES), f32),
            pltpu.VMEM((groups, own_tokens, 2 * own_rows), f32),
            pltpu.VMEM((tokens, 2 * own_rows), bf16),
            pltpu.VMEM((PIECES, steps, layers * own_tokens, piece), bf16),
            pltpu.VMEM((PIECES, steps, layers * own_tokens, piece), bf16),
            pltpu.VMEM((PIECES, layers * own_tokens, piece), f32),
            pltpu.VMEM((PIECES, layers - 1, 2 * own_tokens, half), bf16),
            pltpu.VMEM((PIECES, layers, 2 * own_tokens, half), bf16),
            pltpu.VMEM((PIECES, own_tokens, piece), f32),
            pltpu.VMEM((groups, lines // groups, LANES), f32),
            pltpu.VMEM((2, groups, lines // groups, LANES), f32),
            pltpu.VMEM((groups, lines // groups, LANES), f32),
            dma((len(operands),)),
            dma((2,)),
            dma((PIECES, groups)),
            dma((PIECES, layers)),
            dma((PIECES, layers, PLANE)),
            dma((PIECES, groups)),
            dma((2 * groups,)),
            dma((groups,)),
            dma((2, PIECES, steps)),
            dma((PIECES, layers)),
            dma((PIECES, layers)),
            dma((PIECES,)),
            dma((PIECES,)),
            dma((groups,)),
            dma((2, groups)),
            dma((2 * groups,)),
            dma((groups,)),
        ],
        compiler_params=pltpu.CompilerParams(
            collective_id=0, has_side_effects=True, vmem_limit_bytes=VMEM_BYTES
        ),
    )(*(pltpu.with_memory_space_constraint(item, pltpu.HBM) for item in operands))
    return settle(*results)


def settle_kernel(count, *refs):
    sems = refs[-1]
    copies = [
        pltpu.make_async_copy(refs[index], refs[count + index], sems.at[index])
        for index in range(count)
    ]
    for copy in copies:
        copy.start()
    for copy in copies:
        copy.wait()


def settle(*results):
    count = len(results)
    settled = pl.pallas_call(
        functools.partial(settle_kernel, count),
        out_shape=tuple(jax.ShapeDtypeStruct(x.shape, x.dtype) for x in results),
        in_specs=[pl.BlockSpec(memory_space=pltpu.VMEM)] * count,
        out_specs=(pl.BlockSpec(memory_space=pltpu.HBM),) * count,
        scratch_shapes=[pltpu.SemaphoreType.DMA((count,))],
    )(*(pltpu.with_memory_space_constraint(x, pltpu.VMEM) for x in results))
    grad_hidden, grad_gain, head_new, moment_new, second_new = settled
    return grad_hidden, grad_gain.reshape(-1), head_new, moment_new, second_new.reshape(-1)


def fits(mesh, hidden, head):
    groups, cores = mesh.shape["dp"], mesh.shape["tensor"]
    return (
        cores == 2
        and groups == 4 * PLANE
        and hidden.shape[0] == LANES
        and hidden.shape[1] % (groups * cores * LANES) == 0
        and hidden.shape[0] == groups * 8
        and head.shape[0] == groups * cores * LANES
    )


def solution(mesh):
    placed = (
        P("dp", None),
        P(),
        P(("dp", "tensor"), None),
        P(("dp", "tensor"), None),
        P(("dp", "tensor")),
        P("dp"),
    )

    def whole(hidden, gain, head, moment, second, labels):
        body = local
        if fits(mesh, hidden, head):
            body = functools.partial(fused, mesh.shape["dp"])
        return jax.shard_map(
            body,
            mesh=mesh,
            in_specs=placed,
            out_specs=(
                P("dp", None),
                P(),
                P(("dp", "tensor"), None),
                P(("dp", "tensor"), None),
                P(("dp", "tensor")),
            ),
            check_vma=False,
        )(hidden, gain, head, moment, second, labels)

    return whole
```

```python
import functools

import jax
import jax.numpy as jnp
from jax import lax
from jax.experimental import pallas as pl
from jax.experimental.pallas import tpu as pltpu
from jax.sharding import PartitionSpec as P

MESH = pl.DeviceIdType.MESH
LANES = 128
PLANE = 4
CHUNK = 512
PIECES = 4
STEPS = (3, 1, 2)
LEADS = ((0,), (1, 2, 3))
CHUNK_COUNT = 4
CHUNKS = ((0,), (1, 2, 3))
VMEM_BYTES = 40 * 1024 * 1024

D = 4096


loss_scale = 16.0
beta_one = 0.9
beta_two = 0.999
adam_eps = 1e-08
step_size = 0.02
norm_eps = 1e-05
bias_one = 1.0 - 0.9**10
bias_two = 1.0 - 0.999**10


def inverse_norm(values_f):
    squares = jnp.sum(values_f * values_f, axis=1)
    return lax.rsqrt(squares / D + norm_eps)


def softmax_grad(logits, targets, vocab_ids):
    local_max = jnp.max(logits, axis=1)
    local_sum = jnp.sum(jnp.exp(logits - local_max[:, None]), axis=1)
    global_max = lax.pmax(local_max, ("dp", "tensor"))
    global_sum = lax.psum(local_sum * jnp.exp(local_max - global_max), ("dp", "tensor"))
    onehot = (targets[:, None] == vocab_ids[None, :]).astype(jnp.float32)
    probability = jnp.exp(logits - global_max[:, None]) / global_sum[:, None]
    return (loss_scale * (probability - onehot)).astype(jnp.bfloat16)


def norm_backward(grad_normed, hidden_part, rstd_part, gain_f):
    inner_sums = jnp.sum(grad_normed * gain_f * hidden_part, axis=1)
    return (
        rstd_part[:, None] * gain_f * grad_normed
        - hidden_part * (rstd_part**3)[:, None] * inner_sums[:, None] / D
    ).astype(jnp.bfloat16)


def local(hidden, gain, head, moment, second, labels):
    hidden_f = hidden.astype(jnp.float32)
    gain_f = gain.astype(jnp.float32)
    rstd = inverse_norm(hidden_f)
    normed = (hidden_f * rstd[:, None] * gain_f).astype(jnp.bfloat16)
    normed_all = lax.all_gather(normed, "dp", axis=0, tiled=True)
    all_labels = lax.all_gather(labels, "dp", axis=0, tiled=True)
    own_rows = head.shape[0]
    tensor_count = lax.axis_size("tensor")
    dp_count = lax.axis_size("dp")
    owner = lax.axis_index("dp") * tensor_count + lax.axis_index("tensor")
    vocab_ids = owner * own_rows + jnp.arange(own_rows, dtype=jnp.int32)
    logits = lax.dot_general(
        normed_all, head, (((1,), (1,)), ((), ())), preferred_element_type=jnp.float32
    )
    dlogits = softmax_grad(logits, all_labels, vocab_ids)
    grad_head = lax.dot_general(
        dlogits, normed_all, (((0,), (0,)), ((), ())), preferred_element_type=jnp.float32
    )
    share_rows = hidden.shape[0] // tensor_count
    ordered = dlogits.reshape(dp_count, tensor_count, share_rows, own_rows).transpose(1, 0, 2, 3)
    ordered = ordered.reshape(tensor_count * dp_count * share_rows, own_rows)
    tensor_sum = lax.psum_scatter(
        jnp.dot(ordered, head, preferred_element_type=jnp.float32).astype(jnp.bfloat16),
        "tensor",
        scatter_dimension=0,
        tiled=True,
    ).astype(jnp.float32)
    full_sum = lax.psum(tensor_sum, "dp")
    grad_normed = lax.dynamic_slice_in_dim(
        full_sum, lax.axis_index("dp") * share_rows, share_rows, 0
    )
    offset = lax.axis_index("tensor") * share_rows
    hidden_part = lax.dynamic_slice_in_dim(hidden_f, offset, share_rows, 0)
    rstd_part = lax.dynamic_slice_in_dim(rstd, offset, share_rows, 0)
    grad_gain = lax.psum(
        jnp.sum(grad_normed * hidden_part * rstd_part[:, None], axis=0), ("dp", "tensor")
    )
    part_grad = norm_backward(grad_normed, hidden_part, rstd_part, gain_f)
    grad_hidden = lax.all_gather(part_grad, "tensor", axis=0, tiled=True)
    row_sums = jnp.sum(grad_head * grad_head, axis=1)
    second_new = beta_two * second + (1.0 - beta_two) * row_sums / D
    first = beta_one * moment.astype(jnp.float32) + (1.0 - beta_one) * grad_head
    adam_step = first / bias_one / (jnp.sqrt(second_new / bias_two)[:, None] + adam_eps)
    head_new = (head.astype(jnp.float32) - step_size * adam_step).astype(jnp.bfloat16)
    return (grad_hidden, grad_gain, head_new, first.astype(jnp.bfloat16), second_new)


def wide(values):
    return values.astype(jnp.float32)


def narrow(values):
    return values.astype(jnp.bfloat16)


def fused_kernel(
    layers,
    hidden_hbm,
    gain_hbm,
    head_hbm,
    moment_hbm,
    second_hbm,
    labels_hbm,
    grad_hidden_ref,
    grad_gain_ref,
    head_new,
    moment_new,
    second_out,
    gathered,
    normed,
    hidden,
    gain,
    heads,
    moment,
    second,
    labels,
    gain_wide,
    rates,
    logits_acc,
    grad_head,
    stat_out,
    stat_in,
    token_rows,
    by_token,
    by_row,
    squares,
    plane_out,
    plane_in,
    plane_sum,
    line_out,
    line_in,
    kept,
    final,
    gain_own,
    gain_pair,
    gain_in,
    local_sems,
    gather_send,
    gather_recv,
    block_recv,
    row_recv,
    stat_send,
    plane_recv,
    plane_send,
    line_send,
    line_recv,
    sends,
    recvs,
):
    groups = layers * PLANE
    own_tokens, width = hidden.shape
    own_rows = moment.shape[0]
    tokens = groups * own_tokens
    piece = width // PIECES
    half = piece // 2
    block_cols = width // CHUNK_COUNT
    part_cols = block_cols // 2
    dp = lax.axis_index("dp")
    core = lax.axis_index("tensor")
    layer = lax.div(dp, PLANE)
    spot = lax.rem(dp, PLANE)
    flip = lax.div(layer, 2)
    inward = layer + flip * (3 - 2 * layer)
    pieces = range(PIECES)

    def hop(item):
        if item == layers - 1:
            return layer
        place = 1 - inward if item == 0 else item + 1
        return place + flip * (3 - 2 * place)

    def beside(step):
        down = lax.rem(lax.div(spot, 2) + step // 2, 2)
        return down * 2 + lax.rem(lax.rem(spot, 2) + step % 2, 2)

    def remote(source, target, send_sem, recv_sem, device):
        return pltpu.make_async_remote_copy(
            src_ref=source,
            dst_ref=target,
            send_sem=send_sem,
            recv_sem=recv_sem,
            device_id=device,
            device_id_type=MESH,
        )

    loads = [
        pltpu.make_async_copy(source, target, local_sems.at[index])
        for index, (source, target) in enumerate(
            [
                (hidden_hbm, hidden),
                (gain_hbm, gain),
                (head_hbm, heads.at[core]),
                (labels_hbm, labels),
                (moment_hbm, moment),
                (second_hbm, second),
            ]
        )
    ]
    for load in loads[:2]:
        load.start()

    barrier = pltpu.get_barrier_semaphore()
    nearby = [(hop(item) * PLANE + spot) for item in (2, 1, 0)]
    nearby += [(layer * PLANE + beside(step)) for step in STEPS]

    @pl.when(core == 1)
    def _():
        for group in nearby:
            for to in (1, 0):
                pl.semaphore_signal(barrier, inc=1, device_id=(group, to), device_id_type=MESH)

    pl.semaphore_signal(barrier, inc=1, device_id=(dp, 1 - core), device_id_type=MESH)

    for load in loads[2:]:
        load.start()

    def run(me):
        you = 1 - me
        chunks = CHUNKS[me]
        first, count = chunks[0], len(chunks)
        lead, leads = LEADS[me][0], len(LEADS[me])

        def send(*parts):
            remote(*parts).start()

        def landed(ref, sem):
            remote(ref, ref, sem, sem, (dp, you)).wait_recv()

        def left(ref, sem):
            remote(ref, ref, sem, sem, (dp, you)).wait_send()

        loads[0].wait()
        loads[1].wait()
        gain_rows = wide(gain[...])
        for row in range(width // LANES):
            gain_wide[:, row * LANES : (row + 1) * LANES] = gain_rows[row : row + 1]
        hidden_f = wide(hidden[...])
        rstd = lax.rsqrt(jnp.sum(hidden_f * hidden_f, axis=1, keepdims=True) / width + norm_eps)
        own = hidden_f * rstd * gain_wide[...]
        rates[...] = jnp.broadcast_to(rstd, rates.shape)
        for part in pieces:
            at = part * piece
            gathered[part, dp] = narrow(
                jnp.concatenate([own[:, at : at + half], own[:, at + half : at + piece]], axis=0)
            )
        pl.semaphore_wait(barrier, len(nearby) + 1)

        def group_of(item, step=0):
            return hop(item) * PLANE + (beside(step) if step else spot)

        def shard(part, group, send_sem, recv_sem, device):
            block = gathered.at[part, group]
            send(block, block, send_sem, recv_sem, device)

        def plane_shards(part, item, steps, send_sem):
            for step in steps:
                shard(
                    part,
                    group_of(item),
                    send_sem,
                    block_recv.at[part],
                    (layer * PLANE + beside(step), 1),
                )

        def line_slot(part, away):
            return gather_recv.at[part, lax.rem(away + layers, layers) - 1]

        def ordered(index):
            return lax.rem(index + 1, 3) + lax.div(index, 3) * 2

        def columns(at, size):
            return pl.ds(pl.multiple_of(at, size), size)

        def add_logits(part):
            block = wide(gathered[part]).reshape(groups, 2, own_tokens, half)
            block = [block[:, side].reshape(tokens, half) for side in range(2)]
            block = narrow(jnp.concatenate(block, axis=1))
            normed[part] = block
            logits_acc[...] += lax.dot_general(
                heads[:, :, columns(part * piece, piece)].reshape(2 * own_rows, piece),
                block,
                (((1,), (1,)), ((), ())),
                preferred_element_type=jnp.float32,
            )

        @pl.loop(lead, lead + leads)
        def _(part):
            for item in (2, 1, 0):
                shard(
                    part,
                    dp,
                    gather_send.at[0],
                    line_slot(part, hop(item) - layer),
                    (hop(item) * PLANE + spot, 1),
                )

        if me == 0:

            @pl.loop(0, PIECES)
            def _(part):
                plane_shards(part, 3, STEPS, gather_send.at[1])

        loads[2].wait()
        send(heads.at[me], heads.at[me], sends.at[0], recvs.at[0], (dp, you))
        logits_acc[...] = jnp.zeros_like(logits_acc)

        @pl.loop(0, PIECES)
        def _(index):
            part = ordered(index)
            if me == 0:
                landed(gathered.at[part, pl.ds(0, 2)], row_recv.at[part])
                for item in range(2):
                    plane_shards(part, item, STEPS[:1], gather_send.at[2])
            else:
                for item in range(layers - 1):
                    group = group_of(item)
                    landed(gathered.at[part, group], line_slot(part, layer - hop(item)))
                    plane_shards(part, item, STEPS[1:] if item < 2 else STEPS, gather_send.at[1])
                    shard(
                        part,
                        group,
                        gather_send.at[2],
                        row_recv.at[part] if item < 2 else block_recv.at[part],
                        (dp, you),
                    )

        from_plane = len(STEPS) * layers
        landed(heads.at[you], recvs.at[0])

        @pl.loop(0, PIECES)
        def _(index):
            part = ordered(index)
            landed(gathered.at[part, pl.ds(0, from_plane + you)], block_recv.at[part])
            if me == 1:

                @pl.loop(0, layers)
                def _(row):
                    for step in STEPS:
                        shard(
                            part,
                            row * PLANE + beside(step),
                            gather_send.at[3],
                            block_recv.at[part],
                            (dp, you),
                        )

            add_logits(part)

        logits = logits_acc[...]
        lane = lax.broadcasted_iota(jnp.int32, (1, tokens), 1)

        def far_first(index):
            away = lax.div(index + 1, 2) * (1 - 2 * lax.rem(index, 2))
            return lax.rem(dp + groups // 2 + away, groups)

        def stat_move(group, to_core):
            send(
                stat_out.at[pl.ds(0, 4)],
                stat_in.at[dp, pl.ds(0, 4)],
                stat_send.at[to_core],
                recvs.at[1],
                (group, to_core),
            )

        if me == 1:
            loads[3].wait()
            local_max = jnp.max(logits, axis=0, keepdims=True)
            stat_out[0:1] = local_max
            stat_out[1:2] = jnp.sum(jnp.exp(logits - local_max), axis=0, keepdims=True)
            targets = jnp.zeros((1, tokens), jnp.int32)
            for item in range(own_tokens):
                targets = jnp.where(lane == dp * own_tokens + item, labels[item], targets)
            stat_out[2:3] = wide(targets)
            stat_out[3:4] = jnp.zeros((1, tokens), jnp.float32)

            for to_core in (1, 0):

                @pl.loop(0, groups - 1)
                def _(index):
                    stat_move(far_first(index), to_core)

            stat_move(dp, 0)
            stat_in[dp, 0:4] = stat_out[0:4]
        landed(stat_in.at[pl.ds(0, groups - me), pl.ds(0, 4)], recvs.at[1])
        peaks = stat_in[:, 0, :]
        global_max = jnp.max(peaks, axis=0, keepdims=True)
        global_sum = jnp.sum(stat_in[:, 1, :] * jnp.exp(peaks - global_max), axis=0, keepdims=True)
        all_targets = jnp.sum(stat_in[:, 2, :], axis=0, keepdims=True).astype(jnp.int32)
        vocab = dp * 2 * own_rows + lax.broadcasted_iota(jnp.int32, logits.shape, 0)
        onehot = wide(vocab == all_targets)
        probability = jnp.exp(logits - global_max) / global_sum
        scaled = loss_scale * (probability - onehot)
        token_rows[...] = scaled.T.reshape(groups, own_tokens, 2 * own_rows)
        by_row[...] = narrow(scaled[me * own_rows : (me + 1) * own_rows])
        for index, step in enumerate(STEPS + (0,)):
            blocks = [
                token_rows[hop(item) * PLANE + beside(step)] for item in range(layers)
            ]
            rows = layers * own_tokens
            by_token[index * rows : (index + 1) * rows] = narrow(jnp.concatenate(blocks, axis=0))

        rows = layers * own_tokens

        def scatter(chunk):
            partial = jnp.dot(
                by_token[...],
                heads[:, :, columns(chunk * block_cols, block_cols)].reshape(
                    2 * own_rows, block_cols
                ),
                preferred_element_type=jnp.float32,
            )
            for index in range(len(STEPS)):
                plane_out[chunk, index] = narrow(partial[index * rows : (index + 1) * rows])
            plane_sum[chunk] = partial[len(STEPS) * rows :]
            for index in range(len(STEPS)):
                send(
                    plane_out.at[chunk, index],
                    plane_in.at[chunk, index],
                    plane_send.at[0],
                    plane_recv.at[chunk - first],
                    (layer * PLANE + beside(STEPS[index]), me),
                )

        def head_gradient():
            squares[...] = jnp.zeros_like(squares)

            for index in range(2 * PIECES):
                span = slice(index * half, (index + 1) * half)
                product = jnp.dot(
                    by_row[...],
                    normed[index // 2, :, index % 2 * half : (index % 2 + 1) * half],
                    preferred_element_type=jnp.float32,
                )
                grad_head[:, span] = product
                squares[...] += jnp.sum(product * product, axis=1, keepdims=True)
                shares = jnp.sum(product * wide(heads[me, :, span]), axis=0, keepdims=True)
                shares = shares / gain_wide[:, span]
                for line in range(half // LANES):
                    place = index * (half // LANES) + line
                    gain_own[place : place + 1] = shares[:, line * LANES : (line + 1) * LANES]

        @pl.loop(first, first + count)
        def _(chunk):
            scatter(chunk)

        head_gradient()
        if me == 0:
            send(gain_own, gain_pair, sends.at[2], recvs.at[2], (dp, 1))
        loads[4].wait()
        loads[5].wait()
        second_wide = jnp.broadcast_to(second[...], (LANES, own_rows)).T
        second_new = beta_two * second_wide + (1.0 - beta_two) * squares[:, 0:1] / width
        second_out[...] = second_new.T[0:1, :]
        scale = (step_size / bias_one) / (jnp.sqrt(second_new / bias_two) + adam_eps)
        scale = scale[:, 0:1]

        def adam(index, carry):
            span = pl.ds(pl.multiple_of(index * CHUNK, CHUNK), CHUNK)
            first = beta_one * wide(moment[:, span]) + (1.0 - beta_one) * grad_head[:, span]
            moment_new[:, span] = narrow(first)
            head_new[:, span] = narrow(wide(heads[me, :, span]) - first * scale)
            return carry

        lax.fori_loop(0, width // CHUNK, adam, 0)

        if me == 1:
            landed(gain_pair, recvs.at[2])
            gain_own[...] += gain_pair[...]
            gain_in[dp] = narrow(gain_own[...])

            @pl.loop(0, groups - 1)
            def _(index):
                send(
                    gain_in.at[dp],
                    gain_in.at[dp],
                    sends.at[2],
                    recvs.at[3],
                    (far_first(index), 1),
                )

        @pl.loop(first, first + count)
        def _(chunk):
            landed(plane_in.at[chunk], plane_recv.at[chunk - first])
            total = plane_sum[chunk]
            for index in range(len(STEPS)):
                total = total + wide(plane_in[chunk, index])
            for item in range(layers - 1):
                part = total[item * own_tokens : (item + 1) * own_tokens]
                line_out[chunk, item] = narrow(
                    jnp.concatenate([part[:, :part_cols], part[:, part_cols:]], axis=0)
                )
            for item in (2, 1, 0):
                away = lax.rem(hop(item) - layer + layers, layers) - 1
                send(
                    line_out.at[chunk, item],
                    line_in.at[chunk, away],
                    line_send.at[0],
                    line_recv.at[chunk],
                    (hop(item) * PLANE + spot, 1),
                )
            kept[chunk] = total[(layers - 1) * own_tokens :]
            if me == 0:
                send(kept.at[chunk], kept.at[chunk], sends.at[3 + me], recvs.at[4], (dp, 1))


        if me == 1:
            landed(kept.at[pl.ds(CHUNKS[0][0], len(CHUNKS[0]))], recvs.at[4])

            @pl.loop(0, CHUNK_COUNT)
            def _(index):
                chunk = lax.rem(index + first, CHUNK_COUNT)
                landed(line_in.at[chunk], line_recv.at[chunk])
                total = kept[chunk]
                for item in range(layers - 1):
                    part = wide(line_in[chunk, item])
                    total = total + jnp.concatenate(
                        [part[:own_tokens], part[own_tokens:]], axis=1
                    )
                final[chunk] = total
                send(final.at[chunk], final.at[chunk], sends.at[4], recvs.at[4], (dp, 0))

            landed(gain_in.at[pl.ds(0, groups - 1)], recvs.at[3])
            gain_own[...] = jnp.sum(wide(gain_in[...]), axis=0)
            send(gain_own, gain_pair, sends.at[1], recvs.at[3], (dp, 0))
        else:
            landed(final, recvs.at[4])
        summed = jnp.concatenate([final[chunk] for chunk in range(CHUNK_COUNT)], axis=1) * gain_wide[...]
        hidden_f = wide(hidden[...])
        rstd = rates[:, 0:1]
        inner = jnp.sum(summed * hidden_f, axis=1, keepdims=True)
        grad_hidden_ref[...] = narrow(
            rstd * summed - hidden_f * (rstd * rstd * rstd * inner / width)
        )
        if me == 0:
            landed(gain_pair, recvs.at[3])
        grad_gain_ref[...] = gain_own[...] if me else gain_pair[...]
        if me == 0:
            loads[3].wait()
        own_parts = pl.ds(first, count)
        left(gathered.at[pl.ds(lead, leads), pl.ds(0, layers - 1)], gather_send.at[0])
        left(heads.at[me], sends.at[0])
        left(plane_out.at[own_parts], plane_send.at[0])
        left(line_out.at[own_parts], line_send.at[0])
        if me == 0:
            left(gain_own, sends.at[2])
            left(kept.at[own_parts], sends.at[3])
            left(gathered.at[:, pl.ds(0, len(STEPS))], gather_send.at[1])
            left(gathered.at[:, pl.ds(0, 2)], gather_send.at[2])
        else:
            left(gathered.at[:, pl.ds(0, len(STEPS) + 4)], gather_send.at[1])
            left(gathered.at[:, pl.ds(0, layers - 1)], gather_send.at[2])
            left(gathered.at[:, pl.ds(0, from_plane)], gather_send.at[3])
            for to_core in range(2):
                left(
                    stat_in.at[pl.ds(0, groups - to_core), pl.ds(0, 4)], stat_send.at[to_core]
                )
            left(final, sends.at[4])
            left(gain_in.at[pl.ds(0, groups - 1)], sends.at[2])
            left(gain_own, sends.at[1])

    for index in range(2):
        pl.when(core == index)(functools.partial(run, index))


def fused(groups, hidden, gain, head, moment, second, labels):
    own_tokens, width = hidden.shape
    own_rows = head.shape[0]
    layers = groups // PLANE
    tokens = groups * own_tokens
    piece = width // PIECES
    half = piece // 2
    cols = width // CHUNK_COUNT
    lines = width // LANES
    bf16, f32 = jnp.bfloat16, jnp.float32
    vmem = pl.BlockSpec(memory_space=pltpu.VMEM)
    hbm = pl.BlockSpec(memory_space=pltpu.HBM)
    dma = pltpu.SemaphoreType.DMA
    operands = (
        hidden,
        gain.reshape(lines, LANES),
        head,
        moment,
        second.reshape(1, own_rows),
        labels,
    )
    steps = len(STEPS)
    results = pl.pallas_call(
        functools.partial(fused_kernel, layers),
        out_shape=(
            pltpu.VMEM(hidden.shape, bf16),
            pltpu.VMEM((lines, LANES), f32),
            pltpu.VMEM(head.shape, bf16),
            pltpu.VMEM(head.shape, bf16),
            pltpu.VMEM((1, own_rows), f32),
        ),
        in_specs=[hbm] * len(operands),
        out_specs=(vmem,) * 5,
        scratch_shapes=[
            pltpu.VMEM((PIECES, groups, 2 * own_tokens, half), bf16),
            pltpu.VMEM((PIECES, tokens, piece), bf16),
            pltpu.VMEM(hidden.shape, bf16),
            pltpu.VMEM((lines, LANES), bf16),
            pltpu.VMEM((2, own_rows, width), bf16),
            pltpu.VMEM((own_rows, width), bf16),
            pltpu.VMEM((1, own_rows), f32),
            pltpu.SMEM((own_tokens,), jnp.int32),
            pltpu.VMEM((1, width), f32),
            pltpu.VMEM((own_tokens, LANES), f32),
            pltpu.VMEM((2 * own_rows, tokens), f32),
            pltpu.VMEM((own_rows, width), f32),
            pltpu.VMEM((8, LANES), f32),
            pltpu.VMEM((groups, 8, LANES), f32),
            pltpu.VMEM((groups, own_tokens, 2 * own_rows), f32),
            pltpu.VMEM((tokens, 2 * own_rows), bf16),
            pltpu.VMEM((own_rows, tokens), bf16),
            pltpu.VMEM((own_rows, LANES), f32),
            pltpu.VMEM((CHUNK_COUNT, steps, layers * own_tokens, cols), bf16),
            pltpu.VMEM((CHUNK_COUNT, steps, layers * own_tokens, cols), bf16),
            pltpu.VMEM((CHUNK_COUNT, layers * own_tokens, cols), f32),
            pltpu.VMEM((CHUNK_COUNT, layers - 1, 2 * own_tokens, cols // 2), bf16),
            pltpu.VMEM((CHUNK_COUNT, layers - 1, 2 * own_tokens, cols // 2), bf16),
            pltpu.VMEM((CHUNK_COUNT, own_tokens, cols), f32),
            pltpu.VMEM((CHUNK_COUNT, own_tokens, cols), f32),
            pltpu.VMEM((lines, LANES), f32),
            pltpu.VMEM((lines, LANES), f32),
            pltpu.VMEM((groups, lines, LANES), bf16),
            dma((len(operands),)),
            dma((4,)),
            dma((PIECES, layers - 1)),
            dma((PIECES,)),
            dma((PIECES,)),
            dma((2,)),
            dma((max(len(chunks) for chunks in CHUNKS),)),
            dma((1,)),
            dma((1,)),
            dma((CHUNK_COUNT,)),
            dma((5,)),
            dma((5,)),
        ],
        compiler_params=pltpu.CompilerParams(
            collective_id=0, has_side_effects=True, vmem_limit_bytes=VMEM_BYTES
        ),
    )(*(pltpu.with_memory_space_constraint(item, pltpu.HBM) for item in operands))
    return settle(*results)


def settle_kernel(count, *refs):
    sems = refs[-1]
    copies = [
        pltpu.make_async_copy(refs[index], refs[count + index], sems.at[index])
        for index in range(count)
    ]
    for copy in copies:
        copy.start()
    for copy in copies:
        copy.wait()


def settle(*results):
    count = len(results)
    settled = pl.pallas_call(
        functools.partial(settle_kernel, count),
        out_shape=tuple(jax.ShapeDtypeStruct(x.shape, x.dtype) for x in results),
        in_specs=[pl.BlockSpec(memory_space=pltpu.VMEM)] * count,
        out_specs=(pl.BlockSpec(memory_space=pltpu.HBM),) * count,
        scratch_shapes=[pltpu.SemaphoreType.DMA((count,))],
    )(*(pltpu.with_memory_space_constraint(x, pltpu.VMEM) for x in results))
    grad_hidden, grad_gain, head_new, moment_new, second_new = settled
    return grad_hidden, grad_gain.reshape(-1), head_new, moment_new, second_new.reshape(-1)


def fits(mesh, hidden, head):
    groups, cores = mesh.shape["dp"], mesh.shape["tensor"]
    return (
        cores == 2
        and groups == 4 * PLANE
        and hidden.shape[0] == LANES
        and hidden.shape[1] % (groups * cores * LANES) == 0
        and hidden.shape[0] == groups * 8
        and head.shape[0] == groups * cores * LANES
    )


def solution(mesh):
    placed = (
        P("dp", None),
        P(),
        P(("dp", "tensor"), None),
        P(("dp", "tensor"), None),
        P(("dp", "tensor")),
        P("dp"),
    )

    def whole(hidden, gain, head, moment, second, labels):
        body = local
        if fits(mesh, hidden, head):
            body = functools.partial(fused, mesh.shape["dp"])
        return jax.shard_map(
            body,
            mesh=mesh,
            in_specs=placed,
            out_specs=(
                P("dp", None),
                P(),
                P(("dp", "tensor"), None),
                P(("dp", "tensor"), None),
                P(("dp", "tensor")),
            ),
            check_vma=False,
        )(hidden, gain, head, moment, second, labels)

    return whole
```

```python
import functools

import jax
import jax.numpy as jnp
from jax import lax
from jax.experimental import pallas as pl
from jax.experimental.pallas import tpu as pltpu
from jax.sharding import PartitionSpec as P

MESH = pl.DeviceIdType.MESH
LANES = 128
PLANE = 4
CHUNK = 512
PIECES = 4
STEPS = (3, 1, 2)
LEADS = ((0,), (1, 2, 3))
CHUNK_COUNT = 4
CHUNKS = ((0,), (1, 2, 3))
VMEM_BYTES = 40 * 1024 * 1024

D = 4096


loss_scale = 16.0
beta_one = 0.9
beta_two = 0.999
adam_eps = 1e-08
step_size = 0.02
norm_eps = 1e-05
bias_one = 1.0 - 0.9**10
bias_two = 1.0 - 0.999**10


def inverse_norm(values_f):
    squares = jnp.sum(values_f * values_f, axis=1)
    return lax.rsqrt(squares / D + norm_eps)


def softmax_grad(logits, targets, vocab_ids):
    local_max = jnp.max(logits, axis=1)
    local_sum = jnp.sum(jnp.exp(logits - local_max[:, None]), axis=1)
    global_max = lax.pmax(local_max, ("dp", "tensor"))
    global_sum = lax.psum(local_sum * jnp.exp(local_max - global_max), ("dp", "tensor"))
    onehot = (targets[:, None] == vocab_ids[None, :]).astype(jnp.float32)
    probability = jnp.exp(logits - global_max[:, None]) / global_sum[:, None]
    return (loss_scale * (probability - onehot)).astype(jnp.bfloat16)


def norm_backward(grad_normed, hidden_part, rstd_part, gain_f):
    inner_sums = jnp.sum(grad_normed * gain_f * hidden_part, axis=1)
    return (
        rstd_part[:, None] * gain_f * grad_normed
        - hidden_part * (rstd_part**3)[:, None] * inner_sums[:, None] / D
    ).astype(jnp.bfloat16)


def local(hidden, gain, head, moment, second, labels):
    hidden_f = hidden.astype(jnp.float32)
    gain_f = gain.astype(jnp.float32)
    rstd = inverse_norm(hidden_f)
    normed = (hidden_f * rstd[:, None] * gain_f).astype(jnp.bfloat16)
    normed_all = lax.all_gather(normed, "dp", axis=0, tiled=True)
    all_labels = lax.all_gather(labels, "dp", axis=0, tiled=True)
    own_rows = head.shape[0]
    tensor_count = lax.axis_size("tensor")
    dp_count = lax.axis_size("dp")
    owner = lax.axis_index("dp") * tensor_count + lax.axis_index("tensor")
    vocab_ids = owner * own_rows + jnp.arange(own_rows, dtype=jnp.int32)
    logits = lax.dot_general(
        normed_all, head, (((1,), (1,)), ((), ())), preferred_element_type=jnp.float32
    )
    dlogits = softmax_grad(logits, all_labels, vocab_ids)
    grad_head = lax.dot_general(
        dlogits, normed_all, (((0,), (0,)), ((), ())), preferred_element_type=jnp.float32
    )
    share_rows = hidden.shape[0] // tensor_count
    ordered = dlogits.reshape(dp_count, tensor_count, share_rows, own_rows).transpose(1, 0, 2, 3)
    ordered = ordered.reshape(tensor_count * dp_count * share_rows, own_rows)
    tensor_sum = lax.psum_scatter(
        jnp.dot(ordered, head, preferred_element_type=jnp.float32).astype(jnp.bfloat16),
        "tensor",
        scatter_dimension=0,
        tiled=True,
    ).astype(jnp.float32)
    full_sum = lax.psum(tensor_sum, "dp")
    grad_normed = lax.dynamic_slice_in_dim(
        full_sum, lax.axis_index("dp") * share_rows, share_rows, 0
    )
    offset = lax.axis_index("tensor") * share_rows
    hidden_part = lax.dynamic_slice_in_dim(hidden_f, offset, share_rows, 0)
    rstd_part = lax.dynamic_slice_in_dim(rstd, offset, share_rows, 0)
    grad_gain = lax.psum(
        jnp.sum(grad_normed * hidden_part * rstd_part[:, None], axis=0), ("dp", "tensor")
    )
    part_grad = norm_backward(grad_normed, hidden_part, rstd_part, gain_f)
    grad_hidden = lax.all_gather(part_grad, "tensor", axis=0, tiled=True)
    row_sums = jnp.sum(grad_head * grad_head, axis=1)
    second_new = beta_two * second + (1.0 - beta_two) * row_sums / D
    first = beta_one * moment.astype(jnp.float32) + (1.0 - beta_one) * grad_head
    adam_step = first / bias_one / (jnp.sqrt(second_new / bias_two)[:, None] + adam_eps)
    head_new = (head.astype(jnp.float32) - step_size * adam_step).astype(jnp.bfloat16)
    return (grad_hidden, grad_gain, head_new, first.astype(jnp.bfloat16), second_new)


def wide(values):
    return values.astype(jnp.float32)


def narrow(values):
    return values.astype(jnp.bfloat16)


def fused_kernel(
    layers,
    hidden_hbm,
    gain_hbm,
    head_hbm,
    moment_hbm,
    second_hbm,
    labels_hbm,
    grad_hidden_ref,
    grad_gain_ref,
    head_new,
    moment_new,
    second_out,
    gathered,
    normed,
    hidden,
    gain,
    heads,
    moment,
    second,
    labels,
    gain_wide,
    rates,
    logits_acc,
    grad_head,
    stat_out,
    stat_in,
    token_rows,
    by_token,
    by_row,
    squares,
    plane_out,
    plane_in,
    plane_sum,
    line_out,
    line_in,
    kept,
    final,
    gain_own,
    gain_pair,
    gain_line,
    gain_plane,
    local_sems,
    gather_send,
    gather_recv,
    block_recv,
    row_recv,
    stat_send,
    plane_recv,
    plane_send,
    line_send,
    line_recv,
    gain_recv,
    sends,
    recvs,
):
    groups = layers * PLANE
    own_tokens, width = hidden.shape
    own_rows = moment.shape[0]
    tokens = groups * own_tokens
    piece = width // PIECES
    half = piece // 2
    block_cols = width // CHUNK_COUNT
    part_cols = block_cols // 2
    dp = lax.axis_index("dp")
    core = lax.axis_index("tensor")
    layer = lax.div(dp, PLANE)
    spot = lax.rem(dp, PLANE)
    flip = lax.div(layer, 2)
    inward = layer + flip * (3 - 2 * layer)
    pieces = range(PIECES)

    def hop(item):
        if item == layers - 1:
            return layer
        place = 1 - inward if item == 0 else item + 1
        return place + flip * (3 - 2 * place)

    def beside(step):
        down = lax.rem(lax.div(spot, 2) + step // 2, 2)
        return down * 2 + lax.rem(lax.rem(spot, 2) + step % 2, 2)

    def remote(source, target, send_sem, recv_sem, device):
        return pltpu.make_async_remote_copy(
            src_ref=source,
            dst_ref=target,
            send_sem=send_sem,
            recv_sem=recv_sem,
            device_id=device,
            device_id_type=MESH,
        )

    loads = [
        pltpu.make_async_copy(source, target, local_sems.at[index])
        for index, (source, target) in enumerate(
            [
                (hidden_hbm, hidden),
                (gain_hbm, gain),
                (head_hbm, heads.at[core]),
                (labels_hbm, labels),
                (moment_hbm, moment),
                (second_hbm, second),
            ]
        )
    ]
    for load in loads[:2]:
        load.start()

    barrier = pltpu.get_barrier_semaphore()
    nearby = [(hop(item) * PLANE + spot) for item in (2, 1, 0)]
    nearby += [(layer * PLANE + beside(step)) for step in STEPS]

    @pl.when(core == 1)
    def _():
        for group in nearby:
            for to in (1, 0):
                pl.semaphore_signal(barrier, inc=1, device_id=(group, to), device_id_type=MESH)

    pl.semaphore_signal(barrier, inc=1, device_id=(dp, 1 - core), device_id_type=MESH)

    for load in loads[2:]:
        load.start()

    def run(me):
        you = 1 - me
        chunks = CHUNKS[me]
        first, count = chunks[0], len(chunks)
        lead, leads = LEADS[me][0], len(LEADS[me])

        def send(*parts):
            remote(*parts).start()

        def landed(ref, sem):
            remote(ref, ref, sem, sem, (dp, you)).wait_recv()

        def left(ref, sem):
            remote(ref, ref, sem, sem, (dp, you)).wait_send()

        loads[0].wait()
        loads[1].wait()
        gain_rows = wide(gain[...])
        for row in range(width // LANES):
            gain_wide[:, row * LANES : (row + 1) * LANES] = gain_rows[row : row + 1]
        hidden_f = wide(hidden[...])
        rstd = lax.rsqrt(jnp.sum(hidden_f * hidden_f, axis=1, keepdims=True) / width + norm_eps)
        own = hidden_f * rstd * gain_wide[...]
        rates[...] = jnp.broadcast_to(rstd, rates.shape)
        for part in pieces:
            at = part * piece
            gathered[part, dp] = narrow(
                jnp.concatenate([own[:, at : at + half], own[:, at + half : at + piece]], axis=0)
            )
        pl.semaphore_wait(barrier, len(nearby) + 1)

        def group_of(item, step=0):
            return hop(item) * PLANE + (beside(step) if step else spot)

        def shard(part, group, send_sem, recv_sem, device):
            block = gathered.at[part, group]
            send(block, block, send_sem, recv_sem, device)

        def plane_shards(part, item, steps, send_sem):
            for step in steps:
                shard(
                    part,
                    group_of(item),
                    send_sem,
                    block_recv.at[part],
                    (layer * PLANE + beside(step), 1),
                )

        def line_slot(part, away):
            return gather_recv.at[part, lax.rem(away + layers, layers) - 1]

        def ordered(index):
            return lax.rem(index + 1, 3) + lax.div(index, 3) * 2

        def columns(at, size):
            return pl.ds(pl.multiple_of(at, size), size)

        def add_logits(part):
            block = wide(gathered[part]).reshape(groups, 2, own_tokens, half)
            block = [block[:, side].reshape(tokens, half) for side in range(2)]
            block = narrow(jnp.concatenate(block, axis=1))
            normed[part] = block
            logits_acc[...] += lax.dot_general(
                heads[:, :, columns(part * piece, piece)].reshape(2 * own_rows, piece),
                block,
                (((1,), (1,)), ((), ())),
                preferred_element_type=jnp.float32,
            )

        @pl.loop(lead, lead + leads)
        def _(part):
            for item in (2, 1, 0):
                shard(
                    part,
                    dp,
                    gather_send.at[0],
                    line_slot(part, hop(item) - layer),
                    (hop(item) * PLANE + spot, 1),
                )

        if me == 0:

            @pl.loop(0, PIECES)
            def _(part):
                plane_shards(part, 3, STEPS, gather_send.at[1])

        loads[2].wait()
        send(heads.at[me], heads.at[me], sends.at[0], recvs.at[0], (dp, you))
        logits_acc[...] = jnp.zeros_like(logits_acc)
        if me == 1:
            loads[3].wait()
            lane = lax.broadcasted_iota(jnp.int32, (1, tokens), 1)
            targets = jnp.zeros((1, tokens), jnp.int32)
            for item in range(own_tokens):
                targets = jnp.where(lane == dp * own_tokens + item, labels[item], targets)
            stat_out[2:3] = wide(targets)
            stat_out[3:4] = jnp.zeros((1, tokens), jnp.float32)

        @pl.loop(0, PIECES)
        def _(index):
            part = ordered(index)
            if me == 0:
                landed(gathered.at[part, pl.ds(0, 2)], row_recv.at[part])
                for item in range(2):
                    plane_shards(part, item, STEPS[:1], gather_send.at[2])
            else:
                for item in range(layers - 1):
                    group = group_of(item)
                    landed(gathered.at[part, group], line_slot(part, layer - hop(item)))
                    plane_shards(part, item, STEPS[1:] if item < 2 else STEPS, gather_send.at[1])
                    shard(
                        part,
                        group,
                        gather_send.at[2],
                        row_recv.at[part] if item < 2 else block_recv.at[part],
                        (dp, you),
                    )

        from_plane = len(STEPS) * layers
        landed(heads.at[you], recvs.at[0])

        @pl.loop(0, PIECES)
        def _(index):
            part = ordered(index)
            landed(gathered.at[part, pl.ds(0, from_plane + you)], block_recv.at[part])
            if me == 1:

                @pl.loop(0, layers)
                def _(row):
                    for step in STEPS:
                        shard(
                            part,
                            row * PLANE + beside(step),
                            gather_send.at[3],
                            block_recv.at[part],
                            (dp, you),
                        )

            add_logits(part)

        logits = logits_acc[...]

        def far_first(index):
            away = lax.div(index + 1, 2) * (1 - 2 * lax.rem(index, 2))
            return lax.rem(dp + groups // 2 + away, groups)

        def stat_move(group, to_core):
            send(
                stat_out.at[pl.ds(0, 4)],
                stat_in.at[dp, pl.ds(0, 4)],
                stat_send.at[to_core],
                recvs.at[1],
                (group, to_core),
            )

        if me == 1:
            local_max = jnp.max(logits, axis=0, keepdims=True)
            stat_out[0:1] = local_max
            stat_out[1:2] = jnp.sum(jnp.exp(logits - local_max), axis=0, keepdims=True)

            for to_core in (1, 0):

                @pl.loop(0, groups - 1)
                def _(index):
                    stat_move(far_first(index), to_core)

            stat_move(dp, 0)
            stat_in[dp, 0:4] = stat_out[0:4]
        landed(stat_in.at[pl.ds(0, groups - me), pl.ds(0, 4)], recvs.at[1])
        peaks = stat_in[:, 0, :]
        global_max = jnp.max(peaks, axis=0, keepdims=True)
        global_sum = jnp.sum(stat_in[:, 1, :] * jnp.exp(peaks - global_max), axis=0, keepdims=True)
        all_targets = jnp.sum(stat_in[:, 2, :], axis=0, keepdims=True).astype(jnp.int32)
        vocab = dp * 2 * own_rows + lax.broadcasted_iota(jnp.int32, logits.shape, 0)
        onehot = wide(vocab == all_targets)
        probability = jnp.exp(logits - global_max) / global_sum
        scaled = loss_scale * (probability - onehot)
        token_rows[...] = scaled.T.reshape(groups, own_tokens, 2 * own_rows)
        by_row[...] = narrow(scaled[me * own_rows : (me + 1) * own_rows])
        for index, step in enumerate(STEPS + (0,)):
            blocks = [
                token_rows[hop(item) * PLANE + beside(step)] for item in range(layers)
            ]
            rows = layers * own_tokens
            by_token[index * rows : (index + 1) * rows] = narrow(jnp.concatenate(blocks, axis=0))

        rows = layers * own_tokens

        def scatter(chunk):
            partial = jnp.dot(
                by_token[...],
                heads[:, :, columns(chunk * block_cols, block_cols)].reshape(
                    2 * own_rows, block_cols
                ),
                preferred_element_type=jnp.float32,
            )
            for index in range(len(STEPS)):
                plane_out[chunk, index] = narrow(partial[index * rows : (index + 1) * rows])
            plane_sum[chunk] = partial[len(STEPS) * rows :]
            for index in range(len(STEPS)):
                send(
                    plane_out.at[chunk, index],
                    plane_in.at[chunk, index],
                    plane_send.at[0],
                    plane_recv.at[chunk - first],
                    (layer * PLANE + beside(STEPS[index]), me),
                )

        def head_gradient():
            squares[...] = jnp.zeros_like(squares)

            for index in range(2 * PIECES):
                span = slice(index * half, (index + 1) * half)
                product = jnp.dot(
                    by_row[...],
                    normed[index // 2, :, index % 2 * half : (index % 2 + 1) * half],
                    preferred_element_type=jnp.float32,
                )
                grad_head[:, span] = product
                squares[...] += jnp.sum(product * product, axis=1, keepdims=True)
                shares = jnp.sum(product * wide(heads[me, :, span]), axis=0, keepdims=True)
                shares = shares / gain_wide[:, span]
                for line in range(half // LANES):
                    place = index * (half // LANES) + line
                    gain_own[place : place + 1] = shares[:, line * LANES : (line + 1) * LANES]

        @pl.loop(first, first + count)
        def _(chunk):
            scatter(chunk)

        head_gradient()
        if me == 0:
            send(gain_own, gain_pair, sends.at[2], gain_recv.at[0], (dp, 1))
        loads[4].wait()
        loads[5].wait()
        second_wide = jnp.broadcast_to(second[...], (LANES, own_rows)).T
        second_new = beta_two * second_wide + (1.0 - beta_two) * squares[:, 0:1] / width
        second_out[...] = second_new.T[0:1, :]
        scale = (step_size / bias_one) / (jnp.sqrt(second_new / bias_two) + adam_eps)
        scale = scale[:, 0:1]

        def adam(index, carry):
            span = pl.ds(pl.multiple_of(index * CHUNK, CHUNK), CHUNK)
            first = beta_one * wide(moment[:, span]) + (1.0 - beta_one) * grad_head[:, span]
            moment_new[:, span] = narrow(first)
            head_new[:, span] = narrow(wide(heads[me, :, span]) - first * scale)
            return carry

        lax.fori_loop(0, width // CHUNK, adam, 0)

        if me == 1:
            landed(gain_pair, gain_recv.at[0])
            gain_own[...] += gain_pair[...]
            gain_line[layer] = narrow(gain_own[...])
            for item in (2, 1, 0):
                send(
                    gain_line.at[layer],
                    gain_line.at[layer],
                    sends.at[2],
                    recvs.at[2],
                    (hop(item) * PLANE + spot, 1),
                )

        def share():
            landed(gain_line.at[pl.ds(0, layers - 1)], recvs.at[2])
            gain_plane[spot] = narrow(jnp.sum(wide(gain_line[...]), axis=0))
            for step in STEPS:
                send(
                    gain_plane.at[spot],
                    gain_plane.at[spot],
                    sends.at[3],
                    recvs.at[3],
                    (layer * PLANE + beside(step), 1),
                )

        @pl.loop(first, first + count)
        def _(chunk):
            if me == 1:
                pl.when(chunk == chunks[-1])(share)
            landed(plane_in.at[chunk], plane_recv.at[chunk - first])
            total = plane_sum[chunk]
            for index in range(len(STEPS)):
                total = total + wide(plane_in[chunk, index])
            for item in range(layers - 1):
                part = total[item * own_tokens : (item + 1) * own_tokens]
                line_out[chunk, item] = narrow(
                    jnp.concatenate([part[:, :part_cols], part[:, part_cols:]], axis=0)
                )
            for item in (2, 1, 0):
                away = lax.rem(hop(item) - layer + layers, layers) - 1
                send(
                    line_out.at[chunk, item],
                    line_in.at[chunk, away],
                    line_send.at[0],
                    line_recv.at[chunk],
                    (hop(item) * PLANE + spot, 1),
                )
            kept[chunk] = total[(layers - 1) * own_tokens :]
            if me == 0:
                send(kept.at[chunk], kept.at[chunk], sends.at[3 + me], recvs.at[4], (dp, 1))


        if me == 1:
            landed(kept.at[pl.ds(CHUNKS[0][0], len(CHUNKS[0]))], recvs.at[4])

            @pl.loop(0, CHUNK_COUNT)
            def _(index):
                chunk = lax.rem(index + first, CHUNK_COUNT)
                landed(line_in.at[chunk], line_recv.at[chunk])
                total = kept[chunk]
                for item in range(layers - 1):
                    part = wide(line_in[chunk, item])
                    total = total + jnp.concatenate(
                        [part[:own_tokens], part[own_tokens:]], axis=1
                    )
                final[chunk] = total
                send(final.at[chunk], final.at[chunk], sends.at[4], recvs.at[4], (dp, 0))

            landed(gain_plane.at[pl.ds(0, PLANE - 1)], recvs.at[3])
            gain_own[...] = jnp.sum(wide(gain_plane[...]), axis=0)
            send(gain_own, gain_pair, sends.at[1], recvs.at[3], (dp, 0))
        else:
            landed(final, recvs.at[4])
        summed = jnp.concatenate([final[chunk] for chunk in range(CHUNK_COUNT)], axis=1) * gain_wide[...]
        hidden_f = wide(hidden[...])
        rstd = rates[:, 0:1]
        inner = jnp.sum(summed * hidden_f, axis=1, keepdims=True)
        grad_hidden_ref[...] = narrow(
            rstd * summed - hidden_f * (rstd * rstd * rstd * inner / width)
        )
        if me == 0:
            landed(gain_pair, recvs.at[3])
        grad_gain_ref[...] = gain_own[...] if me else gain_pair[...]
        if me == 0:
            loads[3].wait()
        own_parts = pl.ds(first, count)
        left(gathered.at[pl.ds(lead, leads), pl.ds(0, layers - 1)], gather_send.at[0])
        left(heads.at[me], sends.at[0])
        left(plane_out.at[own_parts], plane_send.at[0])
        left(line_out.at[own_parts], line_send.at[0])
        if me == 0:
            left(gain_own, sends.at[2])
            left(kept.at[own_parts], sends.at[3])
            left(gathered.at[:, pl.ds(0, len(STEPS))], gather_send.at[1])
            left(gathered.at[:, pl.ds(0, 2)], gather_send.at[2])
        else:
            left(gathered.at[:, pl.ds(0, len(STEPS) + 4)], gather_send.at[1])
            left(gathered.at[:, pl.ds(0, layers - 1)], gather_send.at[2])
            left(gathered.at[:, pl.ds(0, from_plane)], gather_send.at[3])
            for to_core in range(2):
                left(
                    stat_in.at[pl.ds(0, groups - to_core), pl.ds(0, 4)], stat_send.at[to_core]
                )
            left(final, sends.at[4])
            left(gain_line.at[pl.ds(0, layers - 1)], sends.at[2])
            left(gain_plane.at[pl.ds(0, PLANE - 1)], sends.at[3])
            left(gain_own, sends.at[1])

    for index in range(2):
        pl.when(core == index)(functools.partial(run, index))


def fused(groups, hidden, gain, head, moment, second, labels):
    own_tokens, width = hidden.shape
    own_rows = head.shape[0]
    layers = groups // PLANE
    tokens = groups * own_tokens
    piece = width // PIECES
    half = piece // 2
    cols = width // CHUNK_COUNT
    lines = width // LANES
    bf16, f32 = jnp.bfloat16, jnp.float32
    vmem = pl.BlockSpec(memory_space=pltpu.VMEM)
    hbm = pl.BlockSpec(memory_space=pltpu.HBM)
    dma = pltpu.SemaphoreType.DMA
    operands = (
        hidden,
        gain.reshape(lines, LANES),
        head,
        moment,
        second.reshape(1, own_rows),
        labels,
    )
    steps = len(STEPS)
    results = pl.pallas_call(
        functools.partial(fused_kernel, layers),
        out_shape=(
            pltpu.VMEM(hidden.shape, bf16),
            pltpu.VMEM((lines, LANES), f32),
            pltpu.VMEM(head.shape, bf16),
            pltpu.VMEM(head.shape, bf16),
            pltpu.VMEM((1, own_rows), f32),
        ),
        in_specs=[hbm] * len(operands),
        out_specs=(vmem,) * 5,
        scratch_shapes=[
            pltpu.VMEM((PIECES, groups, 2 * own_tokens, half), bf16),
            pltpu.VMEM((PIECES, tokens, piece), bf16),
            pltpu.VMEM(hidden.shape, bf16),
            pltpu.VMEM((lines, LANES), bf16),
            pltpu.VMEM((2, own_rows, width), bf16),
            pltpu.VMEM((own_rows, width), bf16),
            pltpu.VMEM((1, own_rows), f32),
            pltpu.SMEM((own_tokens,), jnp.int32),
            pltpu.VMEM((1, width), f32),
            pltpu.VMEM((own_tokens, LANES), f32),
            pltpu.VMEM((2 * own_rows, tokens), f32),
            pltpu.VMEM((own_rows, width), f32),
            pltpu.VMEM((8, LANES), f32),
            pltpu.VMEM((groups, 8, LANES), f32),
            pltpu.VMEM((groups, own_tokens, 2 * own_rows), f32),
            pltpu.VMEM((tokens, 2 * own_rows), bf16),
            pltpu.VMEM((own_rows, tokens), bf16),
            pltpu.VMEM((own_rows, LANES), f32),
            pltpu.VMEM((CHUNK_COUNT, steps, layers * own_tokens, cols), bf16),
            pltpu.VMEM((CHUNK_COUNT, steps, layers * own_tokens, cols), bf16),
            pltpu.VMEM((CHUNK_COUNT, layers * own_tokens, cols), f32),
            pltpu.VMEM((CHUNK_COUNT, layers - 1, 2 * own_tokens, cols // 2), bf16),
            pltpu.VMEM((CHUNK_COUNT, layers - 1, 2 * own_tokens, cols // 2), bf16),
            pltpu.VMEM((CHUNK_COUNT, own_tokens, cols), f32),
            pltpu.VMEM((CHUNK_COUNT, own_tokens, cols), f32),
            pltpu.VMEM((lines, LANES), f32),
            pltpu.VMEM((lines, LANES), f32),
            pltpu.VMEM((layers, lines, LANES), bf16),
            pltpu.VMEM((PLANE, lines, LANES), bf16),
            dma((len(operands),)),
            dma((4,)),
            dma((PIECES, layers - 1)),
            dma((PIECES,)),
            dma((PIECES,)),
            dma((2,)),
            dma((max(len(chunks) for chunks in CHUNKS),)),
            dma((1,)),
            dma((1,)),
            dma((CHUNK_COUNT,)),
            dma((1,)),
            dma((5,)),
            dma((5,)),
        ],
        compiler_params=pltpu.CompilerParams(
            collective_id=0, has_side_effects=True, vmem_limit_bytes=VMEM_BYTES
        ),
    )(*(pltpu.with_memory_space_constraint(item, pltpu.HBM) for item in operands))
    return settle(*results)


def settle_kernel(count, *refs):
    sems = refs[-1]
    copies = [
        pltpu.make_async_copy(refs[index], refs[count + index], sems.at[index])
        for index in range(count)
    ]
    for copy in copies:
        copy.start()
    for copy in copies:
        copy.wait()


def settle(*results):
    count = len(results)
    settled = pl.pallas_call(
        functools.partial(settle_kernel, count),
        out_shape=tuple(jax.ShapeDtypeStruct(x.shape, x.dtype) for x in results),
        in_specs=[pl.BlockSpec(memory_space=pltpu.VMEM)] * count,
        out_specs=(pl.BlockSpec(memory_space=pltpu.HBM),) * count,
        scratch_shapes=[pltpu.SemaphoreType.DMA((count,))],
    )(*(pltpu.with_memory_space_constraint(x, pltpu.VMEM) for x in results))
    grad_hidden, grad_gain, head_new, moment_new, second_new = settled
    return grad_hidden, grad_gain.reshape(-1), head_new, moment_new, second_new.reshape(-1)


def fits(mesh, hidden, head):
    groups, cores = mesh.shape["dp"], mesh.shape["tensor"]
    return (
        cores == 2
        and groups == 4 * PLANE
        and hidden.shape[0] == LANES
        and hidden.shape[1] % (groups * cores * LANES) == 0
        and hidden.shape[0] == groups * 8
        and head.shape[0] == groups * cores * LANES
    )


def solution(mesh):
    placed = (
        P("dp", None),
        P(),
        P(("dp", "tensor"), None),
        P(("dp", "tensor"), None),
        P(("dp", "tensor")),
        P("dp"),
    )

    def whole(hidden, gain, head, moment, second, labels):
        body = local
        if fits(mesh, hidden, head):
            body = functools.partial(fused, mesh.shape["dp"])
        return jax.shard_map(
            body,
            mesh=mesh,
            in_specs=placed,
            out_specs=(
                P("dp", None),
                P(),
                P(("dp", "tensor"), None),
                P(("dp", "tensor"), None),
                P(("dp", "tensor")),
            ),
            check_vma=False,
        )(hidden, gain, head, moment, second, labels)

    return whole
```

```python
import functools

import jax
import jax.numpy as jnp
from jax import lax
from jax.experimental import pallas as pl
from jax.experimental.pallas import tpu as pltpu
from jax.sharding import PartitionSpec as P

MESH = pl.DeviceIdType.MESH
LANES = 128
PLANE = 4
CHUNK = 512
PIECES = 4
STEPS = (3, 1, 2)
LEADS = ((0,), (1, 2, 3))
CHUNK_COUNT = 4
CHUNKS = ((0,), (1, 2, 3))
VMEM_BYTES = 40 * 1024 * 1024

D = 4096


loss_scale = 16.0
beta_one = 0.9
beta_two = 0.999
adam_eps = 1e-08
step_size = 0.02
norm_eps = 1e-05
bias_one = 1.0 - 0.9**10
bias_two = 1.0 - 0.999**10


def inverse_norm(values_f):
    squares = jnp.sum(values_f * values_f, axis=1)
    return lax.rsqrt(squares / D + norm_eps)


def softmax_grad(logits, targets, vocab_ids):
    local_max = jnp.max(logits, axis=1)
    local_sum = jnp.sum(jnp.exp(logits - local_max[:, None]), axis=1)
    global_max = lax.pmax(local_max, ("dp", "tensor"))
    global_sum = lax.psum(local_sum * jnp.exp(local_max - global_max), ("dp", "tensor"))
    onehot = (targets[:, None] == vocab_ids[None, :]).astype(jnp.float32)
    probability = jnp.exp(logits - global_max[:, None]) / global_sum[:, None]
    return (loss_scale * (probability - onehot)).astype(jnp.bfloat16)


def norm_backward(grad_normed, hidden_part, rstd_part, gain_f):
    inner_sums = jnp.sum(grad_normed * gain_f * hidden_part, axis=1)
    return (
        rstd_part[:, None] * gain_f * grad_normed
        - hidden_part * (rstd_part**3)[:, None] * inner_sums[:, None] / D
    ).astype(jnp.bfloat16)


def local(hidden, gain, head, moment, second, labels):
    hidden_f = hidden.astype(jnp.float32)
    gain_f = gain.astype(jnp.float32)
    rstd = inverse_norm(hidden_f)
    normed = (hidden_f * rstd[:, None] * gain_f).astype(jnp.bfloat16)
    normed_all = lax.all_gather(normed, "dp", axis=0, tiled=True)
    all_labels = lax.all_gather(labels, "dp", axis=0, tiled=True)
    own_rows = head.shape[0]
    tensor_count = lax.axis_size("tensor")
    dp_count = lax.axis_size("dp")
    owner = lax.axis_index("dp") * tensor_count + lax.axis_index("tensor")
    vocab_ids = owner * own_rows + jnp.arange(own_rows, dtype=jnp.int32)
    logits = lax.dot_general(
        normed_all, head, (((1,), (1,)), ((), ())), preferred_element_type=jnp.float32
    )
    dlogits = softmax_grad(logits, all_labels, vocab_ids)
    grad_head = lax.dot_general(
        dlogits, normed_all, (((0,), (0,)), ((), ())), preferred_element_type=jnp.float32
    )
    share_rows = hidden.shape[0] // tensor_count
    ordered = dlogits.reshape(dp_count, tensor_count, share_rows, own_rows).transpose(1, 0, 2, 3)
    ordered = ordered.reshape(tensor_count * dp_count * share_rows, own_rows)
    tensor_sum = lax.psum_scatter(
        jnp.dot(ordered, head, preferred_element_type=jnp.float32).astype(jnp.bfloat16),
        "tensor",
        scatter_dimension=0,
        tiled=True,
    ).astype(jnp.float32)
    full_sum = lax.psum(tensor_sum, "dp")
    grad_normed = lax.dynamic_slice_in_dim(
        full_sum, lax.axis_index("dp") * share_rows, share_rows, 0
    )
    offset = lax.axis_index("tensor") * share_rows
    hidden_part = lax.dynamic_slice_in_dim(hidden_f, offset, share_rows, 0)
    rstd_part = lax.dynamic_slice_in_dim(rstd, offset, share_rows, 0)
    grad_gain = lax.psum(
        jnp.sum(grad_normed * hidden_part * rstd_part[:, None], axis=0), ("dp", "tensor")
    )
    part_grad = norm_backward(grad_normed, hidden_part, rstd_part, gain_f)
    grad_hidden = lax.all_gather(part_grad, "tensor", axis=0, tiled=True)
    row_sums = jnp.sum(grad_head * grad_head, axis=1)
    second_new = beta_two * second + (1.0 - beta_two) * row_sums / D
    first = beta_one * moment.astype(jnp.float32) + (1.0 - beta_one) * grad_head
    adam_step = first / bias_one / (jnp.sqrt(second_new / bias_two)[:, None] + adam_eps)
    head_new = (head.astype(jnp.float32) - step_size * adam_step).astype(jnp.bfloat16)
    return (grad_hidden, grad_gain, head_new, first.astype(jnp.bfloat16), second_new)


def wide(values):
    return values.astype(jnp.float32)


def narrow(values):
    return values.astype(jnp.bfloat16)


def fused_kernel(
    layers,
    hidden_hbm,
    gain_hbm,
    head_hbm,
    moment_hbm,
    second_hbm,
    labels_hbm,
    grad_hidden_ref,
    grad_gain_ref,
    head_new,
    moment_new,
    second_out,
    gathered,
    normed,
    hidden,
    gain,
    heads,
    moment,
    second,
    labels,
    gain_wide,
    rates,
    logits_acc,
    grad_head,
    stat_out,
    stat_in,
    token_rows,
    by_token,
    by_row,
    squares,
    plane_out,
    plane_in,
    plane_sum,
    line_out,
    line_in,
    kept,
    final,
    gain_own,
    gain_pair,
    gain_line,
    gain_plane,
    local_sems,
    gather_send,
    gather_recv,
    block_recv,
    row_recv,
    stat_send,
    plane_recv,
    plane_send,
    line_send,
    line_recv,
    gain_recv,
    sends,
    recvs,
):
    groups = layers * PLANE
    own_tokens, width = hidden.shape
    own_rows = moment.shape[0]
    tokens = groups * own_tokens
    piece = width // PIECES
    half = piece // 2
    block_cols = width // CHUNK_COUNT
    part_cols = block_cols // 2
    dp = lax.axis_index("dp")
    core = lax.axis_index("tensor")
    layer = lax.div(dp, PLANE)
    spot = lax.rem(dp, PLANE)
    flip = lax.div(layer, 2)
    inward = layer + flip * (3 - 2 * layer)
    pieces = range(PIECES)

    def hop(item):
        if item == layers - 1:
            return layer
        place = 1 - inward if item == 0 else item + 1
        return place + flip * (3 - 2 * place)

    def beside(step):
        down = lax.rem(lax.div(spot, 2) + step // 2, 2)
        return down * 2 + lax.rem(lax.rem(spot, 2) + step % 2, 2)

    def remote(source, target, send_sem, recv_sem, device):
        return pltpu.make_async_remote_copy(
            src_ref=source,
            dst_ref=target,
            send_sem=send_sem,
            recv_sem=recv_sem,
            device_id=device,
            device_id_type=MESH,
        )

    loads = [
        pltpu.make_async_copy(source, target, local_sems.at[index])
        for index, (source, target) in enumerate(
            [
                (hidden_hbm, hidden),
                (gain_hbm, gain),
                (head_hbm, heads.at[core]),
                (labels_hbm, labels),
                (moment_hbm, moment),
                (second_hbm, second),
            ]
        )
    ]
    for load in loads[:2]:
        load.start()

    barrier = pltpu.get_barrier_semaphore()
    nearby = [(hop(item) * PLANE + spot) for item in (2, 1, 0)]
    nearby += [(layer * PLANE + beside(step)) for step in STEPS]

    @pl.when(core == 1)
    def _():
        for group in nearby:
            for to in (1, 0):
                pl.semaphore_signal(barrier, inc=1, device_id=(group, to), device_id_type=MESH)

    pl.semaphore_signal(barrier, inc=1, device_id=(dp, 1 - core), device_id_type=MESH)

    for load in loads[2:]:
        load.start()

    def run(me):
        you = 1 - me
        chunks = CHUNKS[me]
        first, count = chunks[0], len(chunks)
        lead, leads = LEADS[me][0], len(LEADS[me])

        def send(*parts):
            remote(*parts).start()

        def landed(ref, sem):
            remote(ref, ref, sem, sem, (dp, you)).wait_recv()

        def left(ref, sem):
            remote(ref, ref, sem, sem, (dp, you)).wait_send()

        loads[0].wait()
        loads[1].wait()
        gain_rows = wide(gain[...])
        for row in range(width // LANES):
            gain_wide[:, row * LANES : (row + 1) * LANES] = gain_rows[row : row + 1]
        hidden_f = wide(hidden[...])
        rstd = lax.rsqrt(jnp.sum(hidden_f * hidden_f, axis=1, keepdims=True) / width + norm_eps)
        own = hidden_f * rstd * gain_wide[...]
        rates[...] = jnp.broadcast_to(rstd, rates.shape)
        for part in pieces:
            at = part * piece
            gathered[part, dp] = narrow(
                jnp.concatenate([own[:, at : at + half], own[:, at + half : at + piece]], axis=0)
            )
        pl.semaphore_wait(barrier, len(nearby) + 1)

        def group_of(item, step=0):
            return hop(item) * PLANE + (beside(step) if step else spot)

        def shard(part, group, send_sem, recv_sem, device):
            block = gathered.at[part, group]
            send(block, block, send_sem, recv_sem, device)

        def plane_shards(part, item, steps, send_sem):
            for step in steps:
                shard(
                    part,
                    group_of(item),
                    send_sem,
                    block_recv.at[part],
                    (layer * PLANE + beside(step), 1),
                )

        def line_slot(part, away):
            return gather_recv.at[part, lax.rem(away + layers, layers) - 1]

        def ordered(index):
            return lax.rem(index + 1, 3) + lax.div(index, 3) * 2

        def columns(at, size):
            return pl.ds(pl.multiple_of(at, size), size)

        def add_logits(part):
            block = wide(gathered[part]).reshape(groups, 2, own_tokens, half)
            block = [block[:, side].reshape(tokens, half) for side in range(2)]
            block = narrow(jnp.concatenate(block, axis=1))
            normed[part] = block
            logits_acc[...] += lax.dot_general(
                heads[:, :, columns(part * piece, piece)].reshape(2 * own_rows, piece),
                block,
                (((1,), (1,)), ((), ())),
                preferred_element_type=jnp.float32,
            )

        @pl.loop(lead, lead + leads)
        def _(part):
            for item in (2, 1, 0):
                shard(
                    part,
                    dp,
                    gather_send.at[0],
                    line_slot(part, hop(item) - layer),
                    (hop(item) * PLANE + spot, 1),
                )

        if me == 0:

            @pl.loop(0, PIECES)
            def _(part):
                plane_shards(part, 3, STEPS, gather_send.at[1])

        loads[2].wait()
        send(heads.at[me], heads.at[me], sends.at[0], recvs.at[0], (dp, you))
        logits_acc[...] = jnp.zeros_like(logits_acc)
        if me == 1:
            loads[3].wait()
            lane = lax.broadcasted_iota(jnp.int32, (1, tokens), 1)
            targets = jnp.zeros((1, tokens), jnp.int32)
            for item in range(own_tokens):
                targets = jnp.where(lane == dp * own_tokens + item, labels[item], targets)
            stat_out[2:3] = wide(targets)
            stat_out[3:4] = jnp.zeros((1, tokens), jnp.float32)

        @pl.loop(0, PIECES)
        def _(index):
            part = ordered(index)
            if me == 0:
                landed(gathered.at[part, pl.ds(0, 2)], row_recv.at[part])
                for item in range(2):
                    plane_shards(part, item, STEPS[:1], gather_send.at[2])
            else:
                for item in range(layers - 1):
                    group = group_of(item)
                    landed(gathered.at[part, group], line_slot(part, layer - hop(item)))
                    plane_shards(part, item, STEPS[1:] if item < 2 else STEPS, gather_send.at[1])
                    shard(
                        part,
                        group,
                        gather_send.at[2],
                        row_recv.at[part] if item < 2 else block_recv.at[part],
                        (dp, you),
                    )

        from_plane = len(STEPS) * layers
        landed(heads.at[you], recvs.at[0])

        @pl.loop(0, PIECES)
        def _(index):
            part = ordered(index)
            landed(gathered.at[part, pl.ds(0, from_plane + you)], block_recv.at[part])
            if me == 1:

                @pl.loop(0, layers)
                def _(row):
                    for step in STEPS:
                        shard(
                            part,
                            row * PLANE + beside(step),
                            gather_send.at[3],
                            block_recv.at[part],
                            (dp, you),
                        )

            add_logits(part)

        logits = logits_acc[...]

        def far_first(index):
            away = lax.div(index + 1, 2) * (1 - 2 * lax.rem(index, 2))
            return lax.rem(dp + groups // 2 + away, groups)

        def stat_move(group, to_core):
            send(
                stat_out.at[pl.ds(0, 4)],
                stat_in.at[dp, pl.ds(0, 4)],
                stat_send.at[to_core],
                recvs.at[1],
                (group, to_core),
            )

        if me == 1:
            local_max = jnp.max(logits, axis=0, keepdims=True)
            stat_out[0:1] = local_max
            stat_out[1:2] = jnp.sum(jnp.exp(logits - local_max), axis=0, keepdims=True)

            for to_core in (1, 0):

                @pl.loop(0, groups - 1)
                def _(index):
                    stat_move(far_first(index), to_core)

            stat_move(dp, 0)
            stat_in[dp, 0:4] = stat_out[0:4]
        landed(stat_in.at[pl.ds(0, groups - me), pl.ds(0, 4)], recvs.at[1])
        peaks = stat_in[:, 0, :]
        global_max = jnp.max(peaks, axis=0, keepdims=True)
        global_sum = jnp.sum(stat_in[:, 1, :] * jnp.exp(peaks - global_max), axis=0, keepdims=True)
        all_targets = jnp.sum(stat_in[:, 2, :], axis=0, keepdims=True).astype(jnp.int32)
        vocab = dp * 2 * own_rows + lax.broadcasted_iota(jnp.int32, logits.shape, 0)
        onehot = wide(vocab == all_targets)
        probability = jnp.exp(logits - global_max) / global_sum
        scaled = loss_scale * (probability - onehot)
        token_rows[...] = scaled.T.reshape(groups, own_tokens, 2 * own_rows)
        by_row[...] = narrow(scaled[me * own_rows : (me + 1) * own_rows])
        for index, step in enumerate(STEPS + (0,)):
            blocks = [
                token_rows[hop(item) * PLANE + beside(step)] for item in range(layers)
            ]
            rows = layers * own_tokens
            by_token[index * rows : (index + 1) * rows] = narrow(jnp.concatenate(blocks, axis=0))

        rows = layers * own_tokens

        def away_slot(item):
            return lax.rem(hop(item) - layer + layers, layers) - 1

        def scatter(chunk):
            partial = jnp.dot(
                by_token[...],
                heads[:, :, columns(chunk * block_cols, block_cols)].reshape(
                    2 * own_rows, block_cols
                ),
                preferred_element_type=jnp.float32,
            )
            for index in range(len(STEPS) + 1):
                if me == 1:
                    part = partial[index * rows : (index + 1) * rows]
                else:
                    part = jnp.concatenate(
                        [
                            partial[at * rows + index * own_tokens :][:own_tokens]
                            for at in range(PLANE)
                        ],
                        axis=0,
                    )
                if index < len(STEPS):
                    plane_out[chunk, index] = narrow(part)
                else:
                    plane_sum[chunk] = part
            for index in range(len(STEPS)) if me else (2, 1, 0):
                send(
                    plane_out.at[chunk, index],
                    plane_in.at[chunk, index if me else away_slot(index)],
                    plane_send.at[0],
                    plane_recv.at[chunk - first],
                    (layer * PLANE + beside(STEPS[index]), 1) if me else (group_of(index), 0),
                )

        def head_gradient():
            squares[...] = jnp.zeros_like(squares)

            for index in range(2 * PIECES):
                span = slice(index * half, (index + 1) * half)
                product = jnp.dot(
                    by_row[...],
                    normed[index // 2, :, index % 2 * half : (index % 2 + 1) * half],
                    preferred_element_type=jnp.float32,
                )
                grad_head[:, span] = product
                squares[...] += jnp.sum(product * product, axis=1, keepdims=True)
                shares = jnp.sum(product * wide(heads[me, :, span]), axis=0, keepdims=True)
                shares = shares / gain_wide[:, span]
                for line in range(half // LANES):
                    place = index * (half // LANES) + line
                    gain_own[place : place + 1] = shares[:, line * LANES : (line + 1) * LANES]

        @pl.loop(first, first + count)
        def _(chunk):
            scatter(chunk)

        head_gradient()
        if me == 0:
            send(gain_own, gain_pair, sends.at[2], gain_recv.at[0], (dp, 1))
        loads[4].wait()
        loads[5].wait()
        second_wide = jnp.broadcast_to(second[...], (LANES, own_rows)).T
        second_new = beta_two * second_wide + (1.0 - beta_two) * squares[:, 0:1] / width
        second_out[...] = second_new.T[0:1, :]
        scale = (step_size / bias_one) / (jnp.sqrt(second_new / bias_two) + adam_eps)
        scale = scale[:, 0:1]

        def adam(index, carry):
            span = pl.ds(pl.multiple_of(index * CHUNK, CHUNK), CHUNK)
            first = beta_one * wide(moment[:, span]) + (1.0 - beta_one) * grad_head[:, span]
            moment_new[:, span] = narrow(first)
            head_new[:, span] = narrow(wide(heads[me, :, span]) - first * scale)
            return carry

        lax.fori_loop(0, width // CHUNK, adam, 0)

        if me == 1:
            landed(gain_pair, gain_recv.at[0])
            gain_own[...] += gain_pair[...]
            gain_line[layer] = narrow(gain_own[...])
            for item in (2, 1, 0):
                send(
                    gain_line.at[layer],
                    gain_line.at[layer],
                    sends.at[2],
                    recvs.at[2],
                    (hop(item) * PLANE + spot, 1),
                )

        def share():
            landed(gain_line.at[pl.ds(0, layers - 1)], recvs.at[2])
            gain_plane[spot] = narrow(jnp.sum(wide(gain_line[...]), axis=0))
            for step in STEPS:
                send(
                    gain_plane.at[spot],
                    gain_plane.at[spot],
                    sends.at[3],
                    recvs.at[3],
                    (layer * PLANE + beside(step), 1),
                )

        @pl.loop(first, first + count)
        def _(chunk):
            if me == 1:
                pl.when(chunk == chunks[-1])(share)
            landed(plane_in.at[chunk], plane_recv.at[chunk - first])
            total = plane_sum[chunk]
            for index in range(len(STEPS)):
                total = total + wide(plane_in[chunk, index])
            for item in range(layers - 1):
                part = total[item * own_tokens : (item + 1) * own_tokens]
                line_out[chunk, item] = narrow(
                    jnp.concatenate([part[:, :part_cols], part[:, part_cols:]], axis=0)
                )
            for item in (2, 1, 0) if me else range(len(STEPS)):
                send(
                    line_out.at[chunk, item],
                    line_in.at[chunk, away_slot(item) if me else item],
                    line_send.at[0],
                    line_recv.at[chunk],
                    (group_of(item), 1) if me else (layer * PLANE + beside(STEPS[item]), 1),
                )
            kept[chunk] = total[(layers - 1) * own_tokens :]
            if me == 0:
                send(kept.at[chunk], kept.at[chunk], sends.at[3 + me], recvs.at[4], (dp, 1))


        if me == 1:
            landed(kept.at[pl.ds(CHUNKS[0][0], len(CHUNKS[0]))], recvs.at[4])

            @pl.loop(0, CHUNK_COUNT)
            def _(index):
                chunk = lax.rem(index + first, CHUNK_COUNT)
                landed(line_in.at[chunk], line_recv.at[chunk])
                total = kept[chunk]
                for item in range(layers - 1):
                    part = wide(line_in[chunk, item])
                    total = total + jnp.concatenate(
                        [part[:own_tokens], part[own_tokens:]], axis=1
                    )
                final[chunk] = total
                send(final.at[chunk], final.at[chunk], sends.at[4], recvs.at[4], (dp, 0))

            landed(gain_plane.at[pl.ds(0, PLANE - 1)], recvs.at[3])
            gain_own[...] = jnp.sum(wide(gain_plane[...]), axis=0)
            send(gain_own, gain_pair, sends.at[1], recvs.at[3], (dp, 0))
        else:
            landed(final, recvs.at[4])
        summed = jnp.concatenate([final[chunk] for chunk in range(CHUNK_COUNT)], axis=1) * gain_wide[...]
        hidden_f = wide(hidden[...])
        rstd = rates[:, 0:1]
        inner = jnp.sum(summed * hidden_f, axis=1, keepdims=True)
        grad_hidden_ref[...] = narrow(
            rstd * summed - hidden_f * (rstd * rstd * rstd * inner / width)
        )
        if me == 0:
            landed(gain_pair, recvs.at[3])
        grad_gain_ref[...] = gain_own[...] if me else gain_pair[...]
        if me == 0:
            loads[3].wait()
        own_parts = pl.ds(first, count)
        left(gathered.at[pl.ds(lead, leads), pl.ds(0, layers - 1)], gather_send.at[0])
        left(heads.at[me], sends.at[0])
        left(plane_out.at[own_parts], plane_send.at[0])
        left(line_out.at[own_parts], line_send.at[0])
        if me == 0:
            left(gain_own, sends.at[2])
            left(kept.at[own_parts], sends.at[3])
            left(gathered.at[:, pl.ds(0, len(STEPS))], gather_send.at[1])
            left(gathered.at[:, pl.ds(0, 2)], gather_send.at[2])
        else:
            left(gathered.at[:, pl.ds(0, len(STEPS) + 4)], gather_send.at[1])
            left(gathered.at[:, pl.ds(0, layers - 1)], gather_send.at[2])
            left(gathered.at[:, pl.ds(0, from_plane)], gather_send.at[3])
            for to_core in range(2):
                left(
                    stat_in.at[pl.ds(0, groups - to_core), pl.ds(0, 4)], stat_send.at[to_core]
                )
            left(final, sends.at[4])
            left(gain_line.at[pl.ds(0, layers - 1)], sends.at[2])
            left(gain_plane.at[pl.ds(0, PLANE - 1)], sends.at[3])
            left(gain_own, sends.at[1])

    for index in range(2):
        pl.when(core == index)(functools.partial(run, index))


def fused(groups, hidden, gain, head, moment, second, labels):
    own_tokens, width = hidden.shape
    own_rows = head.shape[0]
    layers = groups // PLANE
    tokens = groups * own_tokens
    piece = width // PIECES
    half = piece // 2
    cols = width // CHUNK_COUNT
    lines = width // LANES
    bf16, f32 = jnp.bfloat16, jnp.float32
    vmem = pl.BlockSpec(memory_space=pltpu.VMEM)
    hbm = pl.BlockSpec(memory_space=pltpu.HBM)
    dma = pltpu.SemaphoreType.DMA
    operands = (
        hidden,
        gain.reshape(lines, LANES),
        head,
        moment,
        second.reshape(1, own_rows),
        labels,
    )
    steps = len(STEPS)
    results = pl.pallas_call(
        functools.partial(fused_kernel, layers),
        out_shape=(
            pltpu.VMEM(hidden.shape, bf16),
            pltpu.VMEM((lines, LANES), f32),
            pltpu.VMEM(head.shape, bf16),
            pltpu.VMEM(head.shape, bf16),
            pltpu.VMEM((1, own_rows), f32),
        ),
        in_specs=[hbm] * len(operands),
        out_specs=(vmem,) * 5,
        scratch_shapes=[
            pltpu.VMEM((PIECES, groups, 2 * own_tokens, half), bf16),
            pltpu.VMEM((PIECES, tokens, piece), bf16),
            pltpu.VMEM(hidden.shape, bf16),
            pltpu.VMEM((lines, LANES), bf16),
            pltpu.VMEM((2, own_rows, width), bf16),
            pltpu.VMEM((own_rows, width), bf16),
            pltpu.VMEM((1, own_rows), f32),
            pltpu.SMEM((own_tokens,), jnp.int32),
            pltpu.VMEM((1, width), f32),
            pltpu.VMEM((own_tokens, LANES), f32),
            pltpu.VMEM((2 * own_rows, tokens), f32),
            pltpu.VMEM((own_rows, width), f32),
            pltpu.VMEM((8, LANES), f32),
            pltpu.VMEM((groups, 8, LANES), f32),
            pltpu.VMEM((groups, own_tokens, 2 * own_rows), f32),
            pltpu.VMEM((tokens, 2 * own_rows), bf16),
            pltpu.VMEM((own_rows, tokens), bf16),
            pltpu.VMEM((own_rows, LANES), f32),
            pltpu.VMEM((CHUNK_COUNT, steps, layers * own_tokens, cols), bf16),
            pltpu.VMEM((CHUNK_COUNT, steps, layers * own_tokens, cols), bf16),
            pltpu.VMEM((CHUNK_COUNT, layers * own_tokens, cols), f32),
            pltpu.VMEM((CHUNK_COUNT, layers - 1, 2 * own_tokens, cols // 2), bf16),
            pltpu.VMEM((CHUNK_COUNT, layers - 1, 2 * own_tokens, cols // 2), bf16),
            pltpu.VMEM((CHUNK_COUNT, own_tokens, cols), f32),
            pltpu.VMEM((CHUNK_COUNT, own_tokens, cols), f32),
            pltpu.VMEM((lines, LANES), f32),
            pltpu.VMEM((lines, LANES), f32),
            pltpu.VMEM((layers, lines, LANES), bf16),
            pltpu.VMEM((PLANE, lines, LANES), bf16),
            dma((len(operands),)),
            dma((4,)),
            dma((PIECES, layers - 1)),
            dma((PIECES,)),
            dma((PIECES,)),
            dma((2,)),
            dma((max(len(chunks) for chunks in CHUNKS),)),
            dma((1,)),
            dma((1,)),
            dma((CHUNK_COUNT,)),
            dma((1,)),
            dma((5,)),
            dma((5,)),
        ],
        compiler_params=pltpu.CompilerParams(
            collective_id=0, has_side_effects=True, vmem_limit_bytes=VMEM_BYTES
        ),
    )(*(pltpu.with_memory_space_constraint(item, pltpu.HBM) for item in operands))
    return settle(*results)


def settle_kernel(count, *refs):
    sems = refs[-1]
    copies = [
        pltpu.make_async_copy(refs[index], refs[count + index], sems.at[index])
        for index in range(count)
    ]
    for copy in copies:
        copy.start()
    for copy in copies:
        copy.wait()


def settle(*results):
    count = len(results)
    settled = pl.pallas_call(
        functools.partial(settle_kernel, count),
        out_shape=tuple(jax.ShapeDtypeStruct(x.shape, x.dtype) for x in results),
        in_specs=[pl.BlockSpec(memory_space=pltpu.VMEM)] * count,
        out_specs=(pl.BlockSpec(memory_space=pltpu.HBM),) * count,
        scratch_shapes=[pltpu.SemaphoreType.DMA((count,))],
    )(*(pltpu.with_memory_space_constraint(x, pltpu.VMEM) for x in results))
    grad_hidden, grad_gain, head_new, moment_new, second_new = settled
    return grad_hidden, grad_gain.reshape(-1), head_new, moment_new, second_new.reshape(-1)


def fits(mesh, hidden, head):
    groups, cores = mesh.shape["dp"], mesh.shape["tensor"]
    return (
        cores == 2
        and groups == 4 * PLANE
        and hidden.shape[0] == LANES
        and hidden.shape[1] % (groups * cores * LANES) == 0
        and hidden.shape[0] == groups * 8
        and head.shape[0] == groups * cores * LANES
    )


def solution(mesh):
    placed = (
        P("dp", None),
        P(),
        P(("dp", "tensor"), None),
        P(("dp", "tensor"), None),
        P(("dp", "tensor")),
        P("dp"),
    )

    def whole(hidden, gain, head, moment, second, labels):
        body = local
        if fits(mesh, hidden, head):
            body = functools.partial(fused, mesh.shape["dp"])
        return jax.shard_map(
            body,
            mesh=mesh,
            in_specs=placed,
            out_specs=(
                P("dp", None),
                P(),
                P(("dp", "tensor"), None),
                P(("dp", "tensor"), None),
                P(("dp", "tensor")),
            ),
            check_vma=False,
        )(hidden, gain, head, moment, second, labels)

    return whole
```

```python
import functools

import jax
import jax.numpy as jnp
from jax import lax
from jax.experimental import pallas as pl
from jax.experimental.pallas import tpu as pltpu
from jax.sharding import PartitionSpec as P

MESH = pl.DeviceIdType.MESH
LANES = 128
PLANE = 4
CHUNK = 512
PIECES = 4
STEPS = (3, 1, 2)
LEADS = ((0,), (1, 2, 3))
CHUNK_COUNT = 4
CHUNKS = ((0,), (1, 2, 3))
VMEM_BYTES = 40 * 1024 * 1024

D = 4096


loss_scale = 16.0
beta_one = 0.9
beta_two = 0.999
adam_eps = 1e-08
step_size = 0.02
norm_eps = 1e-05
bias_one = 1.0 - 0.9**10
bias_two = 1.0 - 0.999**10


def inverse_norm(values_f):
    squares = jnp.sum(values_f * values_f, axis=1)
    return lax.rsqrt(squares / D + norm_eps)


def softmax_grad(logits, targets, vocab_ids):
    local_max = jnp.max(logits, axis=1)
    local_sum = jnp.sum(jnp.exp(logits - local_max[:, None]), axis=1)
    global_max = lax.pmax(local_max, ("dp", "tensor"))
    global_sum = lax.psum(local_sum * jnp.exp(local_max - global_max), ("dp", "tensor"))
    onehot = (targets[:, None] == vocab_ids[None, :]).astype(jnp.float32)
    probability = jnp.exp(logits - global_max[:, None]) / global_sum[:, None]
    return (loss_scale * (probability - onehot)).astype(jnp.bfloat16)


def norm_backward(grad_normed, hidden_part, rstd_part, gain_f):
    inner_sums = jnp.sum(grad_normed * gain_f * hidden_part, axis=1)
    return (
        rstd_part[:, None] * gain_f * grad_normed
        - hidden_part * (rstd_part**3)[:, None] * inner_sums[:, None] / D
    ).astype(jnp.bfloat16)


def local(hidden, gain, head, moment, second, labels):
    hidden_f = hidden.astype(jnp.float32)
    gain_f = gain.astype(jnp.float32)
    rstd = inverse_norm(hidden_f)
    normed = (hidden_f * rstd[:, None] * gain_f).astype(jnp.bfloat16)
    normed_all = lax.all_gather(normed, "dp", axis=0, tiled=True)
    all_labels = lax.all_gather(labels, "dp", axis=0, tiled=True)
    own_rows = head.shape[0]
    tensor_count = lax.axis_size("tensor")
    dp_count = lax.axis_size("dp")
    owner = lax.axis_index("dp") * tensor_count + lax.axis_index("tensor")
    vocab_ids = owner * own_rows + jnp.arange(own_rows, dtype=jnp.int32)
    logits = lax.dot_general(
        normed_all, head, (((1,), (1,)), ((), ())), preferred_element_type=jnp.float32
    )
    dlogits = softmax_grad(logits, all_labels, vocab_ids)
    grad_head = lax.dot_general(
        dlogits, normed_all, (((0,), (0,)), ((), ())), preferred_element_type=jnp.float32
    )
    share_rows = hidden.shape[0] // tensor_count
    ordered = dlogits.reshape(dp_count, tensor_count, share_rows, own_rows).transpose(1, 0, 2, 3)
    ordered = ordered.reshape(tensor_count * dp_count * share_rows, own_rows)
    tensor_sum = lax.psum_scatter(
        jnp.dot(ordered, head, preferred_element_type=jnp.float32).astype(jnp.bfloat16),
        "tensor",
        scatter_dimension=0,
        tiled=True,
    ).astype(jnp.float32)
    full_sum = lax.psum(tensor_sum, "dp")
    grad_normed = lax.dynamic_slice_in_dim(
        full_sum, lax.axis_index("dp") * share_rows, share_rows, 0
    )
    offset = lax.axis_index("tensor") * share_rows
    hidden_part = lax.dynamic_slice_in_dim(hidden_f, offset, share_rows, 0)
    rstd_part = lax.dynamic_slice_in_dim(rstd, offset, share_rows, 0)
    grad_gain = lax.psum(
        jnp.sum(grad_normed * hidden_part * rstd_part[:, None], axis=0), ("dp", "tensor")
    )
    part_grad = norm_backward(grad_normed, hidden_part, rstd_part, gain_f)
    grad_hidden = lax.all_gather(part_grad, "tensor", axis=0, tiled=True)
    row_sums = jnp.sum(grad_head * grad_head, axis=1)
    second_new = beta_two * second + (1.0 - beta_two) * row_sums / D
    first = beta_one * moment.astype(jnp.float32) + (1.0 - beta_one) * grad_head
    adam_step = first / bias_one / (jnp.sqrt(second_new / bias_two)[:, None] + adam_eps)
    head_new = (head.astype(jnp.float32) - step_size * adam_step).astype(jnp.bfloat16)
    return (grad_hidden, grad_gain, head_new, first.astype(jnp.bfloat16), second_new)


def wide(values):
    return values.astype(jnp.float32)


def narrow(values):
    return values.astype(jnp.bfloat16)


def fused_kernel(
    layers,
    hidden_hbm,
    gain_hbm,
    head_hbm,
    moment_hbm,
    second_hbm,
    labels_hbm,
    grad_hidden_ref,
    grad_gain_ref,
    head_new,
    moment_new,
    second_out,
    gathered,
    normed,
    hidden,
    gain,
    heads,
    moment,
    second,
    labels,
    gain_wide,
    rates,
    logits_acc,
    grad_head,
    stat_out,
    stat_in,
    token_rows,
    by_token,
    by_row,
    squares,
    plane_out,
    plane_in,
    plane_sum,
    line_out,
    line_in,
    kept,
    final,
    gain_own,
    gain_pair,
    gain_line,
    gain_plane,
    local_sems,
    gather_send,
    gather_recv,
    block_recv,
    row_recv,
    stat_send,
    plane_recv,
    plane_send,
    line_send,
    line_recv,
    gain_recv,
    sends,
    recvs,
):
    groups = layers * PLANE
    own_tokens, width = hidden.shape
    own_rows = moment.shape[0]
    tokens = groups * own_tokens
    piece = width // PIECES
    half = piece // 2
    block_cols = width // CHUNK_COUNT
    part_cols = block_cols // 2
    dp = lax.axis_index("dp")
    core = lax.axis_index("tensor")
    layer = lax.div(dp, PLANE)
    spot = lax.rem(dp, PLANE)
    flip = lax.div(layer, 2)
    inward = layer + flip * (3 - 2 * layer)
    pieces = range(PIECES)

    def hop(item):
        if item == layers - 1:
            return layer
        place = 1 - inward if item == 0 else item + 1
        return place + flip * (3 - 2 * place)

    def beside(step):
        down = lax.rem(lax.div(spot, 2) + step // 2, 2)
        return down * 2 + lax.rem(lax.rem(spot, 2) + step % 2, 2)

    def remote(source, target, send_sem, recv_sem, device):
        return pltpu.make_async_remote_copy(
            src_ref=source,
            dst_ref=target,
            send_sem=send_sem,
            recv_sem=recv_sem,
            device_id=device,
            device_id_type=MESH,
        )

    loads = [
        pltpu.make_async_copy(source, target, local_sems.at[index])
        for index, (source, target) in enumerate(
            [
                (hidden_hbm, hidden),
                (gain_hbm, gain),
                (head_hbm, heads.at[core]),
                (labels_hbm, labels),
                (moment_hbm, moment),
                (second_hbm, second),
            ]
        )
    ]
    for load in loads[:2]:
        load.start()

    barrier = pltpu.get_barrier_semaphore()
    nearby = [(hop(item) * PLANE + spot) for item in (2, 1, 0)]
    nearby += [(layer * PLANE + beside(step)) for step in STEPS]

    @pl.when(core == 1)
    def _():
        for group in nearby:
            for to in (1, 0):
                pl.semaphore_signal(barrier, inc=1, device_id=(group, to), device_id_type=MESH)

    pl.semaphore_signal(barrier, inc=1, device_id=(dp, 1 - core), device_id_type=MESH)

    for load in loads[2:]:
        load.start()

    def run(me):
        you = 1 - me
        chunks = CHUNKS[me]
        first, count = chunks[0], len(chunks)
        lead, leads = LEADS[me][0], len(LEADS[me])

        def send(*parts):
            remote(*parts).start()

        def landed(ref, sem):
            remote(ref, ref, sem, sem, (dp, you)).wait_recv()

        def left(ref, sem):
            remote(ref, ref, sem, sem, (dp, you)).wait_send()

        loads[0].wait()
        loads[1].wait()
        gain_rows = wide(gain[...])
        for row in range(width // LANES):
            gain_wide[:, row * LANES : (row + 1) * LANES] = gain_rows[row : row + 1]
        hidden_f = wide(hidden[...])
        rstd = lax.rsqrt(jnp.sum(hidden_f * hidden_f, axis=1, keepdims=True) / width + norm_eps)
        own = hidden_f * rstd * gain_wide[...]
        rates[...] = jnp.broadcast_to(rstd, rates.shape)
        for part in pieces:
            at = part * piece
            gathered[part, dp] = narrow(
                jnp.concatenate([own[:, at : at + half], own[:, at + half : at + piece]], axis=0)
            )
        pl.semaphore_wait(barrier, len(nearby) + 1)

        def group_of(item, step=0):
            return hop(item) * PLANE + (beside(step) if step else spot)

        def shard(part, group, send_sem, recv_sem, device):
            block = gathered.at[part, group]
            send(block, block, send_sem, recv_sem, device)

        def plane_shards(part, item, steps, send_sem):
            for step in steps:
                shard(
                    part,
                    group_of(item),
                    send_sem,
                    block_recv.at[part],
                    (layer * PLANE + beside(step), 1),
                )

        def line_slot(part, away):
            return gather_recv.at[part, lax.rem(away + layers, layers) - 1]

        def ordered(index):
            return lax.rem(index + 1, PIECES)

        def columns(at, size):
            return pl.ds(pl.multiple_of(at, size), size)

        def add_logits(part):
            block = wide(gathered[part]).reshape(groups, 2, own_tokens, half)
            block = [block[:, side].reshape(tokens, half) for side in range(2)]
            block = narrow(jnp.concatenate(block, axis=1))
            normed[part] = block
            logits_acc[...] += lax.dot_general(
                heads[:, :, columns(part * piece, piece)].reshape(2 * own_rows, piece),
                block,
                (((1,), (1,)), ((), ())),
                preferred_element_type=jnp.float32,
            )

        if me == 1:
            for step in STEPS:
                shard(
                    0,
                    dp,
                    gather_send.at[4],
                    row_recv.at[0],
                    (layer * PLANE + beside(step), 1),
                )

        @pl.loop(lead, lead + leads)
        def _(part):
            for item in (2, 1, 0):
                shard(
                    part,
                    dp,
                    gather_send.at[0],
                    line_slot(part, hop(item) - layer) if me else block_recv.at[0],
                    (hop(item) * PLANE + spot, 1),
                )

        if me == 0:

            @pl.loop(1, PIECES)
            def _(part):
                plane_shards(part, 3, STEPS, gather_send.at[1])

        loads[2].wait()
        send(heads.at[me], heads.at[me], sends.at[0], recvs.at[0], (dp, you))
        logits_acc[...] = jnp.zeros_like(logits_acc)
        if me == 1:
            loads[3].wait()
            lane = lax.broadcasted_iota(jnp.int32, (1, tokens), 1)
            targets = jnp.zeros((1, tokens), jnp.int32)
            for item in range(own_tokens):
                targets = jnp.where(lane == dp * own_tokens + item, labels[item], targets)
            stat_out[2:3] = wide(targets)
            stat_out[3:4] = jnp.zeros((1, tokens), jnp.float32)

        if me == 1:
            landed(gathered.at[0, pl.ds(0, len(STEPS))], row_recv.at[0])
            for item in (2, 1, 0):
                for step in STEPS:
                    shard(
                        0,
                        group_of(3, step),
                        gather_send.at[4],
                        block_recv.at[0],
                        (hop(item) * PLANE + spot, 1),
                    )
            for step in STEPS:
                shard(0, group_of(3, step), gather_send.at[2], block_recv.at[0], (dp, 0))

        @pl.loop(1, PIECES)
        def _(part):
            if me == 0:
                landed(gathered.at[part, pl.ds(0, 2)], row_recv.at[part])
                for item in range(2):
                    plane_shards(part, item, STEPS[:1], gather_send.at[2])
            else:
                for item in range(layers - 1):
                    group = group_of(item)
                    landed(gathered.at[part, group], line_slot(part, layer - hop(item)))
                    plane_shards(part, item, STEPS[1:] if item < 2 else STEPS, gather_send.at[1])
                    shard(
                        part,
                        group,
                        gather_send.at[2],
                        row_recv.at[part] if item < 2 else block_recv.at[part],
                        (dp, you),
                    )

        from_plane = len(STEPS) * layers
        landed(heads.at[you], recvs.at[0])

        @pl.loop(0, PIECES)
        def _(index):
            part = ordered(index)
            if me == 1:
                landed(gathered.at[part, pl.ds(0, from_plane)], block_recv.at[part])

                def forward(group):
                    shard(part, group, gather_send.at[3], block_recv.at[part], (dp, 0))

                @pl.when(part > 0)
                def _():
                    @pl.loop(0, layers)
                    def _(row):
                        for step in STEPS:
                            forward(row * PLANE + beside(step))

                @pl.when(part == 0)
                def _():
                    for item in range(layers - 1):
                        for place in range(PLANE):
                            forward(hop(item) * PLANE + place)

            else:

                @pl.when(part > 0)
                def _():
                    landed(gathered.at[part, pl.ds(0, from_plane + 1)], block_recv.at[part])

                @pl.when(part == 0)
                def _():
                    landed(
                        gathered.at[part, pl.ds(0, from_plane + len(STEPS))], block_recv.at[part]
                    )

            add_logits(part)

        logits = logits_acc[...]

        def far_first(index):
            away = lax.div(index + 1, 2) * (1 - 2 * lax.rem(index, 2))
            return lax.rem(dp + groups // 2 + away, groups)

        def stat_move(group, to_core):
            send(
                stat_out.at[pl.ds(0, 4)],
                stat_in.at[dp, pl.ds(0, 4)],
                stat_send.at[to_core],
                recvs.at[1],
                (group, to_core),
            )

        if me == 1:
            local_max = jnp.max(logits, axis=0, keepdims=True)
            stat_out[0:1] = local_max
            stat_out[1:2] = jnp.sum(jnp.exp(logits - local_max), axis=0, keepdims=True)

            for to_core in (1, 0):

                @pl.loop(0, groups - 1)
                def _(index):
                    stat_move(far_first(index), to_core)

            stat_move(dp, 0)
            stat_in[dp, 0:4] = stat_out[0:4]
        landed(stat_in.at[pl.ds(0, groups - me), pl.ds(0, 4)], recvs.at[1])
        peaks = stat_in[:, 0, :]
        global_max = jnp.max(peaks, axis=0, keepdims=True)
        global_sum = jnp.sum(stat_in[:, 1, :] * jnp.exp(peaks - global_max), axis=0, keepdims=True)
        all_targets = jnp.sum(stat_in[:, 2, :], axis=0, keepdims=True).astype(jnp.int32)
        vocab = dp * 2 * own_rows + lax.broadcasted_iota(jnp.int32, logits.shape, 0)
        onehot = wide(vocab == all_targets)
        probability = jnp.exp(logits - global_max) / global_sum
        scaled = loss_scale * (probability - onehot)
        token_rows[...] = scaled.T.reshape(groups, own_tokens, 2 * own_rows)
        by_row[...] = narrow(scaled[me * own_rows : (me + 1) * own_rows])
        for index, step in enumerate(STEPS + (0,)):
            blocks = [
                token_rows[hop(item) * PLANE + beside(step)] for item in range(layers)
            ]
            rows = layers * own_tokens
            by_token[index * rows : (index + 1) * rows] = narrow(jnp.concatenate(blocks, axis=0))

        rows = layers * own_tokens

        def away_slot(item):
            return lax.rem(hop(item) - layer + layers, layers) - 1

        def scatter(chunk):
            partial = jnp.dot(
                by_token[...],
                heads[:, :, columns(chunk * block_cols, block_cols)].reshape(
                    2 * own_rows, block_cols
                ),
                preferred_element_type=jnp.float32,
            )
            for index in range(len(STEPS) + 1):
                if me == 1:
                    part = partial[index * rows : (index + 1) * rows]
                else:
                    part = jnp.concatenate(
                        [
                            partial[at * rows + index * own_tokens :][:own_tokens]
                            for at in range(PLANE)
                        ],
                        axis=0,
                    )
                if index < len(STEPS):
                    plane_out[chunk, index] = narrow(part)
                else:
                    plane_sum[chunk] = part
            for index in range(len(STEPS)) if me else (2, 1, 0):
                send(
                    plane_out.at[chunk, index],
                    plane_in.at[chunk, index if me else away_slot(index)],
                    plane_send.at[0],
                    plane_recv.at[chunk - first],
                    (layer * PLANE + beside(STEPS[index]), 1) if me else (group_of(index), 0),
                )

        def head_gradient():
            squares[...] = jnp.zeros_like(squares)

            for index in range(2 * PIECES):
                span = slice(index * half, (index + 1) * half)
                product = jnp.dot(
                    by_row[...],
                    normed[index // 2, :, index % 2 * half : (index % 2 + 1) * half],
                    preferred_element_type=jnp.float32,
                )
                grad_head[:, span] = product
                squares[...] += jnp.sum(product * product, axis=1, keepdims=True)
                shares = jnp.sum(product * wide(heads[me, :, span]), axis=0, keepdims=True)
                shares = shares / gain_wide[:, span]
                for line in range(half // LANES):
                    place = index * (half // LANES) + line
                    gain_own[place : place + 1] = shares[:, line * LANES : (line + 1) * LANES]

        @pl.loop(first, first + count)
        def _(chunk):
            scatter(chunk)

        head_gradient()
        if me == 0:
            send(gain_own, gain_pair, sends.at[2], gain_recv.at[0], (dp, 1))
        loads[4].wait()
        loads[5].wait()
        second_wide = jnp.broadcast_to(second[...], (LANES, own_rows)).T
        second_new = beta_two * second_wide + (1.0 - beta_two) * squares[:, 0:1] / width
        second_out[...] = second_new.T[0:1, :]
        scale = (step_size / bias_one) / (jnp.sqrt(second_new / bias_two) + adam_eps)
        scale = scale[:, 0:1]

        def adam(index, carry):
            span = pl.ds(pl.multiple_of(index * CHUNK, CHUNK), CHUNK)
            first = beta_one * wide(moment[:, span]) + (1.0 - beta_one) * grad_head[:, span]
            moment_new[:, span] = narrow(first)
            head_new[:, span] = narrow(wide(heads[me, :, span]) - first * scale)
            return carry

        lax.fori_loop(0, width // CHUNK, adam, 0)

        if me == 1:
            landed(gain_pair, gain_recv.at[0])
            gain_own[...] += gain_pair[...]
            gain_line[layer] = narrow(gain_own[...])
            for item in (2, 1, 0):
                send(
                    gain_line.at[layer],
                    gain_line.at[layer],
                    sends.at[2],
                    recvs.at[2],
                    (hop(item) * PLANE + spot, 1),
                )

        def share():
            landed(gain_line.at[pl.ds(0, layers - 1)], recvs.at[2])
            gain_plane[spot] = narrow(jnp.sum(wide(gain_line[...]), axis=0))
            for step in STEPS:
                send(
                    gain_plane.at[spot],
                    gain_plane.at[spot],
                    sends.at[3],
                    recvs.at[3],
                    (layer * PLANE + beside(step), 1),
                )

        @pl.loop(first, first + count)
        def _(chunk):
            if me == 1:
                pl.when(chunk == chunks[-1])(share)
            landed(plane_in.at[chunk], plane_recv.at[chunk - first])
            total = plane_sum[chunk]
            for index in range(len(STEPS)):
                total = total + wide(plane_in[chunk, index])
            for item in range(layers - 1):
                part = total[item * own_tokens : (item + 1) * own_tokens]
                line_out[chunk, item] = narrow(
                    jnp.concatenate([part[:, :part_cols], part[:, part_cols:]], axis=0)
                )
            for item in (2, 1, 0) if me else range(len(STEPS)):
                send(
                    line_out.at[chunk, item],
                    line_in.at[chunk, away_slot(item) if me else item],
                    line_send.at[0],
                    line_recv.at[chunk],
                    (group_of(item), 1) if me else (layer * PLANE + beside(STEPS[item]), 1),
                )
            kept[chunk] = total[(layers - 1) * own_tokens :]
            if me == 0:
                send(kept.at[chunk], kept.at[chunk], sends.at[3 + me], recvs.at[4], (dp, 1))


        if me == 1:
            landed(kept.at[pl.ds(CHUNKS[0][0], len(CHUNKS[0]))], recvs.at[4])

            @pl.loop(0, CHUNK_COUNT)
            def _(index):
                chunk = lax.rem(index + first, CHUNK_COUNT)
                landed(line_in.at[chunk], line_recv.at[chunk])
                total = kept[chunk]
                for item in range(layers - 1):
                    part = wide(line_in[chunk, item])
                    total = total + jnp.concatenate(
                        [part[:own_tokens], part[own_tokens:]], axis=1
                    )
                final[chunk] = total
                send(final.at[chunk], final.at[chunk], sends.at[4], recvs.at[4], (dp, 0))

            landed(gain_plane.at[pl.ds(0, PLANE - 1)], recvs.at[3])
            gain_own[...] = jnp.sum(wide(gain_plane[...]), axis=0)
            send(gain_own, gain_pair, sends.at[1], recvs.at[3], (dp, 0))
        else:
            landed(final, recvs.at[4])
        summed = jnp.concatenate([final[chunk] for chunk in range(CHUNK_COUNT)], axis=1) * gain_wide[...]
        hidden_f = wide(hidden[...])
        rstd = rates[:, 0:1]
        inner = jnp.sum(summed * hidden_f, axis=1, keepdims=True)
        grad_hidden_ref[...] = narrow(
            rstd * summed - hidden_f * (rstd * rstd * rstd * inner / width)
        )
        if me == 0:
            landed(gain_pair, recvs.at[3])
        grad_gain_ref[...] = gain_own[...] if me else gain_pair[...]
        if me == 0:
            loads[3].wait()
        own_parts = pl.ds(first, count)
        left(gathered.at[pl.ds(lead, leads), pl.ds(0, layers - 1)], gather_send.at[0])
        left(heads.at[me], sends.at[0])
        left(plane_out.at[own_parts], plane_send.at[0])
        left(line_out.at[own_parts], line_send.at[0])
        if me == 0:
            left(gain_own, sends.at[2])
            left(kept.at[own_parts], sends.at[3])
            left(gathered.at[pl.ds(1, PIECES - 1), pl.ds(0, len(STEPS))], gather_send.at[1])
            left(gathered.at[pl.ds(1, PIECES - 1), pl.ds(0, 2)], gather_send.at[2])
        else:
            left(gathered.at[pl.ds(1, PIECES - 1), pl.ds(0, len(STEPS) + 4)], gather_send.at[1])
            left(gathered.at[0, pl.ds(0, len(STEPS) * layers)], gather_send.at[4])
            left(gathered.at[:, pl.ds(0, layers - 1)], gather_send.at[2])
            left(gathered.at[:, pl.ds(0, from_plane)], gather_send.at[3])
            for to_core in range(2):
                left(
                    stat_in.at[pl.ds(0, groups - to_core), pl.ds(0, 4)], stat_send.at[to_core]
                )
            left(final, sends.at[4])
            left(gain_line.at[pl.ds(0, layers - 1)], sends.at[2])
            left(gain_plane.at[pl.ds(0, PLANE - 1)], sends.at[3])
            left(gain_own, sends.at[1])

    for index in range(2):
        pl.when(core == index)(functools.partial(run, index))


def fused(groups, hidden, gain, head, moment, second, labels):
    own_tokens, width = hidden.shape
    own_rows = head.shape[0]
    layers = groups // PLANE
    tokens = groups * own_tokens
    piece = width // PIECES
    half = piece // 2
    cols = width // CHUNK_COUNT
    lines = width // LANES
    bf16, f32 = jnp.bfloat16, jnp.float32
    vmem = pl.BlockSpec(memory_space=pltpu.VMEM)
    hbm = pl.BlockSpec(memory_space=pltpu.HBM)
    dma = pltpu.SemaphoreType.DMA
    operands = (
        hidden,
        gain.reshape(lines, LANES),
        head,
        moment,
        second.reshape(1, own_rows),
        labels,
    )
    steps = len(STEPS)
    results = pl.pallas_call(
        functools.partial(fused_kernel, layers),
        out_shape=(
            pltpu.VMEM(hidden.shape, bf16),
            pltpu.VMEM((lines, LANES), f32),
            pltpu.VMEM(head.shape, bf16),
            pltpu.VMEM(head.shape, bf16),
            pltpu.VMEM((1, own_rows), f32),
        ),
        in_specs=[hbm] * len(operands),
        out_specs=(vmem,) * 5,
        scratch_shapes=[
            pltpu.VMEM((PIECES, groups, 2 * own_tokens, half), bf16),
            pltpu.VMEM((PIECES, tokens, piece), bf16),
            pltpu.VMEM(hidden.shape, bf16),
            pltpu.VMEM((lines, LANES), bf16),
            pltpu.VMEM((2, own_rows, width), bf16),
            pltpu.VMEM((own_rows, width), bf16),
            pltpu.VMEM((1, own_rows), f32),
            pltpu.SMEM((own_tokens,), jnp.int32),
            pltpu.VMEM((1, width), f32),
            pltpu.VMEM((own_tokens, LANES), f32),
            pltpu.VMEM((2 * own_rows, tokens), f32),
            pltpu.VMEM((own_rows, width), f32),
            pltpu.VMEM((8, LANES), f32),
            pltpu.VMEM((groups, 8, LANES), f32),
            pltpu.VMEM((groups, own_tokens, 2 * own_rows), f32),
            pltpu.VMEM((tokens, 2 * own_rows), bf16),
            pltpu.VMEM((own_rows, tokens), bf16),
            pltpu.VMEM((own_rows, LANES), f32),
            pltpu.VMEM((CHUNK_COUNT, steps, layers * own_tokens, cols), bf16),
            pltpu.VMEM((CHUNK_COUNT, steps, layers * own_tokens, cols), bf16),
            pltpu.VMEM((CHUNK_COUNT, layers * own_tokens, cols), f32),
            pltpu.VMEM((CHUNK_COUNT, layers - 1, 2 * own_tokens, cols // 2), bf16),
            pltpu.VMEM((CHUNK_COUNT, layers - 1, 2 * own_tokens, cols // 2), bf16),
            pltpu.VMEM((CHUNK_COUNT, own_tokens, cols), f32),
            pltpu.VMEM((CHUNK_COUNT, own_tokens, cols), f32),
            pltpu.VMEM((lines, LANES), f32),
            pltpu.VMEM((lines, LANES), f32),
            pltpu.VMEM((layers, lines, LANES), bf16),
            pltpu.VMEM((PLANE, lines, LANES), bf16),
            dma((len(operands),)),
            dma((5,)),
            dma((PIECES, layers - 1)),
            dma((PIECES,)),
            dma((PIECES,)),
            dma((2,)),
            dma((max(len(chunks) for chunks in CHUNKS),)),
            dma((1,)),
            dma((1,)),
            dma((CHUNK_COUNT,)),
            dma((1,)),
            dma((5,)),
            dma((5,)),
        ],
        compiler_params=pltpu.CompilerParams(
            collective_id=0, has_side_effects=True, vmem_limit_bytes=VMEM_BYTES
        ),
    )(*(pltpu.with_memory_space_constraint(item, pltpu.HBM) for item in operands))
    return settle(*results)


def settle_kernel(count, *refs):
    sems = refs[-1]
    copies = [
        pltpu.make_async_copy(refs[index], refs[count + index], sems.at[index])
        for index in range(count)
    ]
    for copy in copies:
        copy.start()
    for copy in copies:
        copy.wait()


def settle(*results):
    count = len(results)
    settled = pl.pallas_call(
        functools.partial(settle_kernel, count),
        out_shape=tuple(jax.ShapeDtypeStruct(x.shape, x.dtype) for x in results),
        in_specs=[pl.BlockSpec(memory_space=pltpu.VMEM)] * count,
        out_specs=(pl.BlockSpec(memory_space=pltpu.HBM),) * count,
        scratch_shapes=[pltpu.SemaphoreType.DMA((count,))],
    )(*(pltpu.with_memory_space_constraint(x, pltpu.VMEM) for x in results))
    grad_hidden, grad_gain, head_new, moment_new, second_new = settled
    return grad_hidden, grad_gain.reshape(-1), head_new, moment_new, second_new.reshape(-1)


def fits(mesh, hidden, head):
    groups, cores = mesh.shape["dp"], mesh.shape["tensor"]
    return (
        cores == 2
        and groups == 4 * PLANE
        and hidden.shape[0] == LANES
        and hidden.shape[1] % (groups * cores * LANES) == 0
        and hidden.shape[0] == groups * 8
        and head.shape[0] == groups * cores * LANES
    )


def solution(mesh):
    placed = (
        P("dp", None),
        P(),
        P(("dp", "tensor"), None),
        P(("dp", "tensor"), None),
        P(("dp", "tensor")),
        P("dp"),
    )

    def whole(hidden, gain, head, moment, second, labels):
        body = local
        if fits(mesh, hidden, head):
            body = functools.partial(fused, mesh.shape["dp"])
        return jax.shard_map(
            body,
            mesh=mesh,
            in_specs=placed,
            out_specs=(
                P("dp", None),
                P(),
                P(("dp", "tensor"), None),
                P(("dp", "tensor"), None),
                P(("dp", "tensor")),
            ),
            check_vma=False,
        )(hidden, gain, head, moment, second, labels)

    return whole
```

```python
import functools

import jax
import jax.numpy as jnp
from jax import lax
from jax.experimental import pallas as pl
from jax.experimental.pallas import tpu as pltpu
from jax.sharding import PartitionSpec as P

MESH = pl.DeviceIdType.MESH
LANES = 128
PLANE = 4
CHUNK = 512
PIECES = 4
STEPS = (3, 1, 2)
LEADS = ((0,), (1, 2, 3))
CHUNK_COUNT = 4
CHUNKS = ((0,), (1, 2, 3))
VMEM_BYTES = 40 * 1024 * 1024

D = 4096


loss_scale = 16.0
beta_one = 0.9
beta_two = 0.999
adam_eps = 1e-08
step_size = 0.02
norm_eps = 1e-05
bias_one = 1.0 - 0.9**10
bias_two = 1.0 - 0.999**10


def inverse_norm(values_f):
    squares = jnp.sum(values_f * values_f, axis=1)
    return lax.rsqrt(squares / D + norm_eps)


def softmax_grad(logits, targets, vocab_ids):
    local_max = jnp.max(logits, axis=1)
    local_sum = jnp.sum(jnp.exp(logits - local_max[:, None]), axis=1)
    global_max = lax.pmax(local_max, ("dp", "tensor"))
    global_sum = lax.psum(local_sum * jnp.exp(local_max - global_max), ("dp", "tensor"))
    onehot = (targets[:, None] == vocab_ids[None, :]).astype(jnp.float32)
    probability = jnp.exp(logits - global_max[:, None]) / global_sum[:, None]
    return (loss_scale * (probability - onehot)).astype(jnp.bfloat16)


def norm_backward(grad_normed, hidden_part, rstd_part, gain_f):
    inner_sums = jnp.sum(grad_normed * gain_f * hidden_part, axis=1)
    return (
        rstd_part[:, None] * gain_f * grad_normed
        - hidden_part * (rstd_part**3)[:, None] * inner_sums[:, None] / D
    ).astype(jnp.bfloat16)


def local(hidden, gain, head, moment, second, labels):
    hidden_f = hidden.astype(jnp.float32)
    gain_f = gain.astype(jnp.float32)
    rstd = inverse_norm(hidden_f)
    normed = (hidden_f * rstd[:, None] * gain_f).astype(jnp.bfloat16)
    normed_all = lax.all_gather(normed, "dp", axis=0, tiled=True)
    all_labels = lax.all_gather(labels, "dp", axis=0, tiled=True)
    own_rows = head.shape[0]
    tensor_count = lax.axis_size("tensor")
    dp_count = lax.axis_size("dp")
    owner = lax.axis_index("dp") * tensor_count + lax.axis_index("tensor")
    vocab_ids = owner * own_rows + jnp.arange(own_rows, dtype=jnp.int32)
    logits = lax.dot_general(
        normed_all, head, (((1,), (1,)), ((), ())), preferred_element_type=jnp.float32
    )
    dlogits = softmax_grad(logits, all_labels, vocab_ids)
    grad_head = lax.dot_general(
        dlogits, normed_all, (((0,), (0,)), ((), ())), preferred_element_type=jnp.float32
    )
    share_rows = hidden.shape[0] // tensor_count
    ordered = dlogits.reshape(dp_count, tensor_count, share_rows, own_rows).transpose(1, 0, 2, 3)
    ordered = ordered.reshape(tensor_count * dp_count * share_rows, own_rows)
    tensor_sum = lax.psum_scatter(
        jnp.dot(ordered, head, preferred_element_type=jnp.float32).astype(jnp.bfloat16),
        "tensor",
        scatter_dimension=0,
        tiled=True,
    ).astype(jnp.float32)
    full_sum = lax.psum(tensor_sum, "dp")
    grad_normed = lax.dynamic_slice_in_dim(
        full_sum, lax.axis_index("dp") * share_rows, share_rows, 0
    )
    offset = lax.axis_index("tensor") * share_rows
    hidden_part = lax.dynamic_slice_in_dim(hidden_f, offset, share_rows, 0)
    rstd_part = lax.dynamic_slice_in_dim(rstd, offset, share_rows, 0)
    grad_gain = lax.psum(
        jnp.sum(grad_normed * hidden_part * rstd_part[:, None], axis=0), ("dp", "tensor")
    )
    part_grad = norm_backward(grad_normed, hidden_part, rstd_part, gain_f)
    grad_hidden = lax.all_gather(part_grad, "tensor", axis=0, tiled=True)
    row_sums = jnp.sum(grad_head * grad_head, axis=1)
    second_new = beta_two * second + (1.0 - beta_two) * row_sums / D
    first = beta_one * moment.astype(jnp.float32) + (1.0 - beta_one) * grad_head
    adam_step = first / bias_one / (jnp.sqrt(second_new / bias_two)[:, None] + adam_eps)
    head_new = (head.astype(jnp.float32) - step_size * adam_step).astype(jnp.bfloat16)
    return (grad_hidden, grad_gain, head_new, first.astype(jnp.bfloat16), second_new)


def wide(values):
    return values.astype(jnp.float32)


def narrow(values):
    return values.astype(jnp.bfloat16)


def fused_kernel(
    layers,
    hidden_hbm,
    gain_hbm,
    head_hbm,
    moment_hbm,
    second_hbm,
    labels_hbm,
    grad_hidden_ref,
    grad_gain_ref,
    head_new,
    moment_new,
    second_out,
    gathered,
    normed,
    hidden,
    gain,
    heads,
    moment,
    second,
    labels,
    gain_wide,
    rates,
    logits_acc,
    grad_head,
    stat_out,
    stat_in,
    token_rows,
    by_token,
    by_row,
    squares,
    plane_out,
    plane_in,
    plane_sum,
    line_out,
    line_in,
    kept,
    final,
    gain_own,
    gain_pair,
    gain_line,
    gain_plane,
    local_sems,
    gather_send,
    gather_recv,
    block_recv,
    row_recv,
    stat_send,
    plane_recv,
    plane_send,
    line_send,
    line_recv,
    gain_recv,
    sends,
    recvs,
):
    groups = layers * PLANE
    own_tokens, width = hidden.shape
    own_rows = moment.shape[0]
    tokens = groups * own_tokens
    piece = width // PIECES
    half = piece // 2
    block_cols = width // CHUNK_COUNT
    part_cols = block_cols // 2
    dp = lax.axis_index("dp")
    core = lax.axis_index("tensor")
    layer = lax.div(dp, PLANE)
    spot = lax.rem(dp, PLANE)
    flip = lax.div(layer, 2)
    inward = layer + flip * (3 - 2 * layer)
    pieces = range(PIECES)

    def hop(item):
        if item == layers - 1:
            return layer
        place = 1 - inward if item == 0 else item + 1
        return place + flip * (3 - 2 * place)

    def beside(step):
        down = lax.rem(lax.div(spot, 2) + step // 2, 2)
        return down * 2 + lax.rem(lax.rem(spot, 2) + step % 2, 2)

    def remote(source, target, send_sem, recv_sem, device):
        return pltpu.make_async_remote_copy(
            src_ref=source,
            dst_ref=target,
            send_sem=send_sem,
            recv_sem=recv_sem,
            device_id=device,
            device_id_type=MESH,
        )

    loads = [
        pltpu.make_async_copy(source, target, local_sems.at[index])
        for index, (source, target) in enumerate(
            [
                (hidden_hbm, hidden),
                (gain_hbm, gain),
                (head_hbm, heads.at[core]),
                (labels_hbm, labels),
                (moment_hbm, moment),
                (second_hbm, second),
            ]
        )
    ]
    for load in loads[:2]:
        load.start()

    barrier = pltpu.get_barrier_semaphore()
    nearby = [(hop(item) * PLANE + spot) for item in (2, 1, 0)]
    nearby += [(layer * PLANE + beside(step)) for step in STEPS]

    @pl.when(core == 1)
    def _():
        for group in nearby:
            for to in (1, 0):
                pl.semaphore_signal(barrier, inc=1, device_id=(group, to), device_id_type=MESH)

    pl.semaphore_signal(barrier, inc=1, device_id=(dp, 1 - core), device_id_type=MESH)

    for load in loads[2:]:
        load.start()

    def run(me):
        you = 1 - me
        chunks = CHUNKS[me]
        first, count = chunks[0], len(chunks)
        lead, leads = LEADS[me][0], len(LEADS[me])

        def send(*parts):
            remote(*parts).start()

        def landed(ref, sem):
            remote(ref, ref, sem, sem, (dp, you)).wait_recv()

        def left(ref, sem):
            remote(ref, ref, sem, sem, (dp, you)).wait_send()

        loads[0].wait()
        loads[1].wait()
        gain_rows = wide(gain[...])
        for row in range(width // LANES):
            gain_wide[:, row * LANES : (row + 1) * LANES] = gain_rows[row : row + 1]
        hidden_f = wide(hidden[...])
        rstd = lax.rsqrt(jnp.sum(hidden_f * hidden_f, axis=1, keepdims=True) / width + norm_eps)
        own = hidden_f * rstd * gain_wide[...]
        rates[...] = jnp.broadcast_to(rstd, rates.shape)
        for part in pieces:
            at = part * piece
            gathered[part, dp] = narrow(
                jnp.concatenate([own[:, at : at + half], own[:, at + half : at + piece]], axis=0)
            )
        pl.semaphore_wait(barrier, len(nearby) + 1)

        def group_of(item, step=0):
            return hop(item) * PLANE + (beside(step) if step else spot)

        def shard(part, group, send_sem, recv_sem, device):
            block = gathered.at[part, group]
            send(block, block, send_sem, recv_sem, device)

        def plane_shards(part, item, steps, send_sem):
            for step in steps:
                shard(
                    part,
                    group_of(item),
                    send_sem,
                    block_recv.at[part],
                    (layer * PLANE + beside(step), 1),
                )

        def line_slot(part, away):
            return gather_recv.at[part, lax.rem(away + layers, layers) - 1]

        def columns(at, size):
            return pl.ds(pl.multiple_of(at, size), size)

        def add_logits(part):
            block = wide(gathered[part]).reshape(groups, 2, own_tokens, half)
            block = [block[:, side].reshape(tokens, half) for side in range(2)]
            block = narrow(jnp.concatenate(block, axis=1))
            normed[part] = block
            logits_acc[...] += lax.dot_general(
                heads[:, :, columns(part * piece, piece)].reshape(2 * own_rows, piece),
                block,
                (((1,), (1,)), ((), ())),
                preferred_element_type=jnp.float32,
            )

        if me == 1:
            for step in STEPS:
                shard(
                    0,
                    dp,
                    gather_send.at[4],
                    row_recv.at[0],
                    (layer * PLANE + beside(step), 1),
                )

        @pl.loop(lead, lead + leads)
        def _(part):
            for item in (2, 1, 0):
                shard(
                    part,
                    dp,
                    gather_send.at[0],
                    line_slot(part, hop(item) - layer) if me else block_recv.at[0],
                    (hop(item) * PLANE + spot, 1),
                )

        if me == 0:

            @pl.loop(1, PIECES)
            def _(part):
                plane_shards(part, 3, STEPS, gather_send.at[1])

        loads[2].wait()
        send(heads.at[me], heads.at[me], sends.at[0], recvs.at[0], (dp, you))
        logits_acc[...] = jnp.zeros_like(logits_acc)
        if me == 1:
            loads[3].wait()
            lane = lax.broadcasted_iota(jnp.int32, (1, tokens), 1)
            targets = jnp.zeros((1, tokens), jnp.int32)
            for item in range(own_tokens):
                targets = jnp.where(lane == dp * own_tokens + item, labels[item], targets)
            stat_out[2:3] = wide(targets)
            stat_out[3:4] = jnp.zeros((1, tokens), jnp.float32)

        if me == 1:
            landed(gathered.at[0, pl.ds(0, len(STEPS))], row_recv.at[0])
            for item in (2, 1, 0):
                for step in STEPS:
                    shard(
                        0,
                        group_of(3, step),
                        gather_send.at[4],
                        block_recv.at[0],
                        (hop(item) * PLANE + spot, 1),
                    )
            for step in STEPS:
                shard(0, group_of(3, step), gather_send.at[2], block_recv.at[0], (dp, 0))

        @pl.loop(1, PIECES)
        def _(part):
            if me == 0:
                landed(gathered.at[part, pl.ds(0, 2)], row_recv.at[part])
                for item in range(2):
                    plane_shards(part, item, STEPS[:1], gather_send.at[2])
            else:
                for item in range(layers - 1):
                    group = group_of(item)
                    landed(gathered.at[part, group], line_slot(part, layer - hop(item)))
                    plane_shards(part, item, STEPS[1:] if item < 2 else STEPS, gather_send.at[1])
                    shard(
                        part,
                        group,
                        gather_send.at[2],
                        row_recv.at[part] if item < 2 else block_recv.at[part],
                        (dp, you),
                    )

        from_plane = len(STEPS) * layers
        landed(heads.at[you], recvs.at[0])

        @pl.loop(0, PIECES)
        def _(part):
            if me == 1:
                landed(gathered.at[part, pl.ds(0, from_plane)], block_recv.at[part])

                def forward(group):
                    shard(part, group, gather_send.at[3], block_recv.at[part], (dp, 0))

                @pl.when(part > 0)
                def _():
                    @pl.loop(0, layers)
                    def _(row):
                        for step in STEPS:
                            forward(row * PLANE + beside(step))

                @pl.when(part == 0)
                def _():
                    for item in range(layers - 1):
                        for place in range(PLANE):
                            forward(hop(item) * PLANE + place)

            else:

                @pl.when(part > 0)
                def _():
                    landed(gathered.at[part, pl.ds(0, from_plane + 1)], block_recv.at[part])

                @pl.when(part == 0)
                def _():
                    landed(
                        gathered.at[part, pl.ds(0, from_plane + len(STEPS))], block_recv.at[part]
                    )

            add_logits(part)

        logits = logits_acc[...]

        def far_first(index):
            away = lax.div(index + 1, 2) * (1 - 2 * lax.rem(index, 2))
            return lax.rem(dp + groups // 2 + away, groups)

        def stat_move(group, to_core):
            send(
                stat_out.at[pl.ds(0, 4)],
                stat_in.at[dp, pl.ds(0, 4)],
                stat_send.at[to_core],
                recvs.at[1],
                (group, to_core),
            )

        if me == 1:
            local_max = jnp.max(logits, axis=0, keepdims=True)
            stat_out[0:1] = local_max
            stat_out[1:2] = jnp.sum(jnp.exp(logits - local_max), axis=0, keepdims=True)

            for to_core in (1, 0):

                @pl.loop(0, groups - 1)
                def _(index):
                    stat_move(far_first(index), to_core)

            stat_move(dp, 0)
            stat_in[dp, 0:4] = stat_out[0:4]
        landed(stat_in.at[pl.ds(0, groups - me), pl.ds(0, 4)], recvs.at[1])
        peaks = stat_in[:, 0, :]
        global_max = jnp.max(peaks, axis=0, keepdims=True)
        global_sum = jnp.sum(stat_in[:, 1, :] * jnp.exp(peaks - global_max), axis=0, keepdims=True)
        all_targets = jnp.sum(stat_in[:, 2, :], axis=0, keepdims=True).astype(jnp.int32)
        vocab = dp * 2 * own_rows + lax.broadcasted_iota(jnp.int32, logits.shape, 0)
        onehot = wide(vocab == all_targets)
        probability = jnp.exp(logits - global_max) / global_sum
        scaled = loss_scale * (probability - onehot)
        token_rows[...] = scaled.T.reshape(groups, own_tokens, 2 * own_rows)
        by_row[...] = narrow(scaled[me * own_rows : (me + 1) * own_rows])
        for index, step in enumerate(STEPS + (0,)):
            blocks = [
                token_rows[hop(item) * PLANE + beside(step)] for item in range(layers)
            ]
            rows = layers * own_tokens
            by_token[index * rows : (index + 1) * rows] = narrow(jnp.concatenate(blocks, axis=0))

        rows = layers * own_tokens

        def away_slot(item):
            return lax.rem(hop(item) - layer + layers, layers) - 1

        def scatter(chunk):
            partial = jnp.dot(
                by_token[...],
                heads[:, :, columns(chunk * block_cols, block_cols)].reshape(
                    2 * own_rows, block_cols
                ),
                preferred_element_type=jnp.float32,
            )
            for index in range(len(STEPS) + 1):
                if me == 1:
                    part = partial[index * rows : (index + 1) * rows]
                else:
                    part = jnp.concatenate(
                        [
                            partial[at * rows + index * own_tokens :][:own_tokens]
                            for at in range(PLANE)
                        ],
                        axis=0,
                    )
                if index < len(STEPS):
                    plane_out[chunk, index] = narrow(part)
                else:
                    plane_sum[chunk] = part
            for index in range(len(STEPS)) if me else (2, 1, 0):
                send(
                    plane_out.at[chunk, index],
                    plane_in.at[chunk, index if me else away_slot(index)],
                    plane_send.at[0],
                    plane_recv.at[chunk - first],
                    (layer * PLANE + beside(STEPS[index]), 1) if me else (group_of(index), 0),
                )

        def head_gradient():
            squares[...] = jnp.zeros_like(squares)

            for index in range(2 * PIECES):
                span = slice(index * half, (index + 1) * half)
                product = jnp.dot(
                    by_row[...],
                    normed[index // 2, :, index % 2 * half : (index % 2 + 1) * half],
                    preferred_element_type=jnp.float32,
                )
                grad_head[:, span] = product
                squares[...] += jnp.sum(product * product, axis=1, keepdims=True)
                shares = jnp.sum(product * wide(heads[me, :, span]), axis=0, keepdims=True)
                shares = shares / gain_wide[:, span]
                for line in range(half // LANES):
                    place = index * (half // LANES) + line
                    gain_own[place : place + 1] = shares[:, line * LANES : (line + 1) * LANES]

        @pl.loop(first, first + count)
        def _(chunk):
            scatter(chunk)

        head_gradient()
        if me == 0:
            send(gain_own, gain_pair, sends.at[2], gain_recv.at[0], (dp, 1))
        loads[4].wait()
        loads[5].wait()
        second_wide = jnp.broadcast_to(second[...], (LANES, own_rows)).T
        second_new = beta_two * second_wide + (1.0 - beta_two) * squares[:, 0:1] / width
        second_out[...] = second_new.T[0:1, :]
        scale = (step_size / bias_one) / (jnp.sqrt(second_new / bias_two) + adam_eps)
        scale = scale[:, 0:1]

        def adam(index, carry):
            span = pl.ds(pl.multiple_of(index * CHUNK, CHUNK), CHUNK)
            first = beta_one * wide(moment[:, span]) + (1.0 - beta_one) * grad_head[:, span]
            moment_new[:, span] = narrow(first)
            head_new[:, span] = narrow(wide(heads[me, :, span]) - first * scale)
            return carry

        lax.fori_loop(0, width // CHUNK, adam, 0)

        if me == 1:
            landed(gain_pair, gain_recv.at[0])
            gain_own[...] += gain_pair[...]
            gain_line[layer] = narrow(gain_own[...])
            for item in (2, 1, 0):
                send(
                    gain_line.at[layer],
                    gain_line.at[layer],
                    sends.at[2],
                    recvs.at[2],
                    (hop(item) * PLANE + spot, 1),
                )

        def share():
            landed(gain_line.at[pl.ds(0, layers - 1)], recvs.at[2])
            gain_plane[spot] = narrow(jnp.sum(wide(gain_line[...]), axis=0))
            for step in STEPS:
                send(
                    gain_plane.at[spot],
                    gain_plane.at[spot],
                    sends.at[3],
                    recvs.at[3],
                    (layer * PLANE + beside(step), 1),
                )

        @pl.loop(first, first + count)
        def _(chunk):
            if me == 1:
                pl.when(chunk == chunks[-1])(share)
            landed(plane_in.at[chunk], plane_recv.at[chunk - first])
            total = plane_sum[chunk]
            for index in range(len(STEPS)):
                total = total + wide(plane_in[chunk, index])
            for item in range(layers - 1):
                part = total[item * own_tokens : (item + 1) * own_tokens]
                line_out[chunk, item] = narrow(
                    jnp.concatenate([part[:, :part_cols], part[:, part_cols:]], axis=0)
                )
            for item in (2, 1, 0) if me else range(len(STEPS)):
                send(
                    line_out.at[chunk, item],
                    line_in.at[chunk, away_slot(item) if me else item],
                    line_send.at[0],
                    line_recv.at[chunk],
                    (group_of(item), 1) if me else (layer * PLANE + beside(STEPS[item]), 1),
                )
            kept[chunk] = total[(layers - 1) * own_tokens :]
            if me == 0:
                send(kept.at[chunk], kept.at[chunk], sends.at[3 + me], recvs.at[4], (dp, 1))


        if me == 1:
            landed(kept.at[pl.ds(CHUNKS[0][0], len(CHUNKS[0]))], recvs.at[4])

            @pl.loop(0, CHUNK_COUNT)
            def _(index):
                chunk = lax.rem(index + first, CHUNK_COUNT)
                landed(line_in.at[chunk], line_recv.at[chunk])
                total = kept[chunk]
                for item in range(layers - 1):
                    part = wide(line_in[chunk, item])
                    total = total + jnp.concatenate(
                        [part[:own_tokens], part[own_tokens:]], axis=1
                    )
                final[chunk] = total
                send(final.at[chunk], final.at[chunk], sends.at[4], recvs.at[4], (dp, 0))

            landed(gain_plane.at[pl.ds(0, PLANE - 1)], recvs.at[3])
            gain_own[...] = jnp.sum(wide(gain_plane[...]), axis=0)
            send(gain_own, gain_pair, sends.at[1], recvs.at[3], (dp, 0))
        else:
            landed(final, recvs.at[4])
        summed = jnp.concatenate([final[chunk] for chunk in range(CHUNK_COUNT)], axis=1) * gain_wide[...]
        hidden_f = wide(hidden[...])
        rstd = rates[:, 0:1]
        inner = jnp.sum(summed * hidden_f, axis=1, keepdims=True)
        grad_hidden_ref[...] = narrow(
            rstd * summed - hidden_f * (rstd * rstd * rstd * inner / width)
        )
        if me == 0:
            landed(gain_pair, recvs.at[3])
        grad_gain_ref[...] = gain_own[...] if me else gain_pair[...]
        if me == 0:
            loads[3].wait()
        own_parts = pl.ds(first, count)
        left(gathered.at[pl.ds(lead, leads), pl.ds(0, layers - 1)], gather_send.at[0])
        left(heads.at[me], sends.at[0])
        left(plane_out.at[own_parts], plane_send.at[0])
        left(line_out.at[own_parts], line_send.at[0])
        if me == 0:
            left(gain_own, sends.at[2])
            left(kept.at[own_parts], sends.at[3])
            left(gathered.at[pl.ds(1, PIECES - 1), pl.ds(0, len(STEPS))], gather_send.at[1])
            left(gathered.at[pl.ds(1, PIECES - 1), pl.ds(0, 2)], gather_send.at[2])
        else:
            left(gathered.at[pl.ds(1, PIECES - 1), pl.ds(0, len(STEPS) + 4)], gather_send.at[1])
            left(gathered.at[0, pl.ds(0, len(STEPS) * layers)], gather_send.at[4])
            left(gathered.at[:, pl.ds(0, layers - 1)], gather_send.at[2])
            left(gathered.at[:, pl.ds(0, from_plane)], gather_send.at[3])
            for to_core in range(2):
                left(
                    stat_in.at[pl.ds(0, groups - to_core), pl.ds(0, 4)], stat_send.at[to_core]
                )
            left(final, sends.at[4])
            left(gain_line.at[pl.ds(0, layers - 1)], sends.at[2])
            left(gain_plane.at[pl.ds(0, PLANE - 1)], sends.at[3])
            left(gain_own, sends.at[1])

    for index in range(2):
        pl.when(core == index)(functools.partial(run, index))


def fused(groups, hidden, gain, head, moment, second, labels):
    own_tokens, width = hidden.shape
    own_rows = head.shape[0]
    layers = groups // PLANE
    tokens = groups * own_tokens
    piece = width // PIECES
    half = piece // 2
    cols = width // CHUNK_COUNT
    lines = width // LANES
    bf16, f32 = jnp.bfloat16, jnp.float32
    vmem = pl.BlockSpec(memory_space=pltpu.VMEM)
    hbm = pl.BlockSpec(memory_space=pltpu.HBM)
    dma = pltpu.SemaphoreType.DMA
    operands = (
        hidden,
        gain.reshape(lines, LANES),
        head,
        moment,
        second.reshape(1, own_rows),
        labels,
    )
    steps = len(STEPS)
    results = pl.pallas_call(
        functools.partial(fused_kernel, layers),
        out_shape=(
            pltpu.VMEM(hidden.shape, bf16),
            pltpu.VMEM((lines, LANES), f32),
            pltpu.VMEM(head.shape, bf16),
            pltpu.VMEM(head.shape, bf16),
            pltpu.VMEM((1, own_rows), f32),
        ),
        in_specs=[hbm] * len(operands),
        out_specs=(vmem,) * 5,
        scratch_shapes=[
            pltpu.VMEM((PIECES, groups, 2 * own_tokens, half), bf16),
            pltpu.VMEM((PIECES, tokens, piece), bf16),
            pltpu.VMEM(hidden.shape, bf16),
            pltpu.VMEM((lines, LANES), bf16),
            pltpu.VMEM((2, own_rows, width), bf16),
            pltpu.VMEM((own_rows, width), bf16),
            pltpu.VMEM((1, own_rows), f32),
            pltpu.SMEM((own_tokens,), jnp.int32),
            pltpu.VMEM((1, width), f32),
            pltpu.VMEM((own_tokens, LANES), f32),
            pltpu.VMEM((2 * own_rows, tokens), f32),
            pltpu.VMEM((own_rows, width), f32),
            pltpu.VMEM((8, LANES), f32),
            pltpu.VMEM((groups, 8, LANES), f32),
            pltpu.VMEM((groups, own_tokens, 2 * own_rows), f32),
            pltpu.VMEM((tokens, 2 * own_rows), bf16),
            pltpu.VMEM((own_rows, tokens), bf16),
            pltpu.VMEM((own_rows, LANES), f32),
            pltpu.VMEM((CHUNK_COUNT, steps, layers * own_tokens, cols), bf16),
            pltpu.VMEM((CHUNK_COUNT, steps, layers * own_tokens, cols), bf16),
            pltpu.VMEM((CHUNK_COUNT, layers * own_tokens, cols), f32),
            pltpu.VMEM((CHUNK_COUNT, layers - 1, 2 * own_tokens, cols // 2), bf16),
            pltpu.VMEM((CHUNK_COUNT, layers - 1, 2 * own_tokens, cols // 2), bf16),
            pltpu.VMEM((CHUNK_COUNT, own_tokens, cols), f32),
            pltpu.VMEM((CHUNK_COUNT, own_tokens, cols), f32),
            pltpu.VMEM((lines, LANES), f32),
            pltpu.VMEM((lines, LANES), f32),
            pltpu.VMEM((layers, lines, LANES), bf16),
            pltpu.VMEM((PLANE, lines, LANES), bf16),
            dma((len(operands),)),
            dma((5,)),
            dma((PIECES, layers - 1)),
            dma((PIECES,)),
            dma((PIECES,)),
            dma((2,)),
            dma((max(len(chunks) for chunks in CHUNKS),)),
            dma((1,)),
            dma((1,)),
            dma((CHUNK_COUNT,)),
            dma((1,)),
            dma((5,)),
            dma((5,)),
        ],
        compiler_params=pltpu.CompilerParams(
            collective_id=0, has_side_effects=True, vmem_limit_bytes=VMEM_BYTES
        ),
    )(*(pltpu.with_memory_space_constraint(item, pltpu.HBM) for item in operands))
    return settle(*results)


def settle_kernel(count, *refs):
    sems = refs[-1]
    copies = [
        pltpu.make_async_copy(refs[index], refs[count + index], sems.at[index])
        for index in range(count)
    ]
    for copy in copies:
        copy.start()
    for copy in copies:
        copy.wait()


def settle(*results):
    count = len(results)
    settled = pl.pallas_call(
        functools.partial(settle_kernel, count),
        out_shape=tuple(jax.ShapeDtypeStruct(x.shape, x.dtype) for x in results),
        in_specs=[pl.BlockSpec(memory_space=pltpu.VMEM)] * count,
        out_specs=(pl.BlockSpec(memory_space=pltpu.HBM),) * count,
        scratch_shapes=[pltpu.SemaphoreType.DMA((count,))],
    )(*(pltpu.with_memory_space_constraint(x, pltpu.VMEM) for x in results))
    grad_hidden, grad_gain, head_new, moment_new, second_new = settled
    return grad_hidden, grad_gain.reshape(-1), head_new, moment_new, second_new.reshape(-1)


def fits(mesh, hidden, head):
    groups, cores = mesh.shape["dp"], mesh.shape["tensor"]
    return (
        cores == 2
        and groups == 4 * PLANE
        and hidden.shape[0] == LANES
        and hidden.shape[1] % (groups * cores * LANES) == 0
        and hidden.shape[0] == groups * 8
        and head.shape[0] == groups * cores * LANES
    )


def solution(mesh):
    placed = (
        P("dp", None),
        P(),
        P(("dp", "tensor"), None),
        P(("dp", "tensor"), None),
        P(("dp", "tensor")),
        P("dp"),
    )

    def whole(hidden, gain, head, moment, second, labels):
        body = local
        if fits(mesh, hidden, head):
            body = functools.partial(fused, mesh.shape["dp"])
        return jax.shard_map(
            body,
            mesh=mesh,
            in_specs=placed,
            out_specs=(
                P("dp", None),
                P(),
                P(("dp", "tensor"), None),
                P(("dp", "tensor"), None),
                P(("dp", "tensor")),
            ),
            check_vma=False,
        )(hidden, gain, head, moment, second, labels)

    return whole
```
